256 devices in a mesh: dev: 256 (over z, y, x, core).
Axes of the slice: x: 4, y: 4, z: 8, core: 2. Of those that a mesh axis runs over, the one named last changes fastest.
Arguments:
- left_table: float32 [524288, 256], P('dev'), may hold values from -6 to 6
- left_state: float32 [524288], P('dev'), may hold values from 0.001 to 0.1
- right_table: float32 [524288, 256], P('dev'), may hold values from -6 to 6
- right_state: float32 [524288], P('dev'), may hold values from 0.001 to 0.1
- relations: float32 [4, 256, 256], replicated, may hold values from -0.375 to 0.375
- relation_state: float32 [4, 256], replicated, may hold values from 6553 to 655360
- edge_weights: int32 [256, 4, 16, 128, 128], P('dev'), may hold values from 0 to 3
- tile_left: int32 [256, 4, 16], P('dev'), may hold values from 0 to 15
- tile_right: int32 [256, 4, 16], P('dev'), may hold values from 0 to 15
- tile_relation: int32 [256, 4, 16], P('dev'), may hold values from 0 to 3
- live_count: int32 [256, 4], P('dev'), may hold values from 2 to 16, as said below
Outputs:
- left_out: float32 [524288, 256], P('dev')
- left_state_out: float32 [524288], P('dev')
- right_out: float32 [524288, 256], P('dev')
- right_state_out: float32 [524288], P('dev')
- relations_out: float32 [4, 256, 256], replicated
- relation_state_out: float32 [4, 256], replicated
The draws below stay inside these ranges and needn't reach their ends.
Inputs may be any that keep to these rules, and one draw needn't show every extreme that they name: `live_count`: in round 0 some partition has exactly 16 live slots.
All inputs are finite; a program needn't handle non-finite values.
Results may differ from the reference program's by a relative error of at most 0.0003.
Values sent between devices are 32-bit elements; how exact they have to be, the bound alone decides.
A program may use at most 128 MiB of HBM per device.

```python
import math
import jax
import jax.numpy as jnp
from jax import lax

D = 256
RELS = 4
TILE = 128
ROWS = 2048
ROUNDS = 4
ACTIVE = 16
PARTITIONS = 256
TILES = 16
TABLE_ROWS = 524288


def draw_live_count(key, part):
    key_first, key_second, key_mark = jax.random.split(jax.random.fold_in(key, 17), 3)
    first = jax.random.randint(key_first, (PARTITIONS, ROUNDS), 0, ACTIVE)
    second = jax.random.randint(key_second, (PARTITIONS, ROUNDS), 0, ACTIVE)
    counted = 2 + (first * second + ACTIVE // 2) // ACTIVE
    counted = jnp.minimum(counted, ACTIVE)
    marked = jax.random.randint(key_mark, (), 0, PARTITIONS)
    spot = (jnp.arange(PARTITIONS)[:, None] == marked) & (jnp.arange(ROUNDS)[None, :] == 0)
    return jnp.where(spot, ACTIVE, counted).astype(jnp.int32)


def set_ends(drawn, stream_key, least, high):
    longest = drawn.shape.index(max(drawn.shape))
    spots = []
    for shift in (0, 1):
        where = [jax.random.randint(jax.random.fold_in(stream_key, axis), (), 0, length) for axis, length in enumerate(drawn.shape)]
        where[longest] = (where[longest] + shift) % drawn.shape[longest]
        spots.append(tuple(where))
    return drawn.at[spots[0]].set(least).at[spots[1]].set(high)


def block_scale(key, dims, shards, least, top_value):
    def one(dim, shards_of):
        draws = jax.random.uniform(jax.random.fold_in(jax.random.fold_in(key, 6), dim), (shards_of,), jnp.float32, least / len(shards), top_value / len(shards))
        return jnp.repeat(jnp.exp(draws), dims[dim] // shards_of).reshape((-1,) + (1,) * (len(dims) - dim - 1))

    level = one(*shards[0])
    for cut in shards[1:]:
        level = level * one(*cut)
    return level


def normal_values(stream_key, shape, width, reach, cuts=(), kind=jnp.bfloat16):
    values = jax.random.normal(stream_key, shape, jnp.float32) * width
    if len(cuts) > 0:
        values = block_scale(stream_key, shape, cuts, -0.22, 0.18) * values
    return jnp.clip(values, min=-reach, max=reach).astype(kind)


def setup_inputs(seed: int = 0) -> dict:
    splits = jax.random.split(jax.random.key(seed), 12)
    left_table = normal_values(splits[0], (TABLE_ROWS, D), 1.0, 6.0, ((0, 256),), jnp.float32)
    left_state = jnp.clip(jnp.exp(math.log(0.1) - 4.6051702 * jax.random.uniform(splits[1], (TABLE_ROWS,), jnp.float32) ** block_scale(splits[1], (TABLE_ROWS,), ((0, 256),), -0.2, 0.2)), 0.001, 0.1)
    right_table = normal_values(splits[2], (TABLE_ROWS, D), 1.0, 6.0, ((0, 256),), jnp.float32)
    right_state = jnp.clip(jnp.exp(math.log(0.1) - 4.6051702 * jax.random.uniform(splits[3], (TABLE_ROWS,), jnp.float32) ** block_scale(splits[3], (TABLE_ROWS,), ((0, 256),), -0.2, 0.2)), 0.001, 0.1)
    relations = normal_values(splits[4], (RELS, D, D), D ** -0.5, 0.375, (), jnp.float32)
    relation_state = jnp.clip(jnp.exp(jax.random.uniform(splits[5], (RELS, D), jnp.float32, math.log(6553.0), math.log(655360.0))), 6553.0, 655360.0)
    edge_weights = set_ends(jax.random.randint(splits[6], (PARTITIONS, ROUNDS, ACTIVE, TILE, TILE), 0, 4), jax.random.fold_in(splits[6], 1), 0, 3).astype(jnp.int32)
    tile_left = set_ends(jax.random.randint(splits[7], (PARTITIONS, ROUNDS, ACTIVE), 0, TILES), jax.random.fold_in(splits[7], 1), 0, TILES - 1).astype(jnp.int32)
    tile_right = set_ends(jax.random.randint(splits[8], (PARTITIONS, ROUNDS, ACTIVE), 0, TILES), jax.random.fold_in(splits[8], 1), 0, TILES - 1).astype(jnp.int32)
    tile_relation = set_ends(jax.random.randint(splits[9], (PARTITIONS, ROUNDS, ACTIVE), 0, RELS), jax.random.fold_in(splits[9], 1), 0, RELS - 1).astype(jnp.int32)
    live_count = draw_live_count(jax.random.fold_in(splits[11], 71), 0)
    return dict(left_table=left_table, left_state=left_state, right_table=right_table, right_state=right_state, relations=relations, relation_state=relation_state, edge_weights=edge_weights, tile_left=tile_left, tile_right=tile_right, tile_relation=tile_relation, live_count=live_count)


HIGHEST = lax.Precision.HIGHEST
learn_rate = 0.1
epsilon = 1e-06
weight_scale = 3.0

def slot_terms(rows_a, rows_b, relation_map, weights):
    scale = D ** (-0.5)
    projected = jnp.dot(rows_a, relation_map, precision=HIGHEST)
    scores = jnp.dot(projected, rows_b.T, precision=HIGHEST) * scale
    positive = weights.astype(scores.dtype) / weight_scale
    negative = (weights == 0).astype(scores.dtype)
    dscore = (negative * jax.nn.sigmoid(scores) - positive * jax.nn.sigmoid(-scores)) * scale
    term_b = jnp.dot(dscore.T, projected, precision=HIGHEST)
    backed = jnp.dot(dscore, rows_b, precision=HIGHEST)
    term_a = jnp.dot(backed, relation_map.T, precision=HIGHEST)
    term_rel = jnp.dot(rows_a.T, backed, precision=HIGHEST)
    return (term_a, term_b, term_rel)

def bucket_grads(table_a, table_b, relations, edges, lefts, rights, kinds, count):

    def add_slot(index, grads):
        grad_a, grad_b, grad_rel = grads
        start_a = (lefts[index] * TILE).astype(jnp.int32)
        start_b = (rights[index] * TILE).astype(jnp.int32)
        rows_a = lax.dynamic_slice_in_dim(table_a, start_a, TILE, 0)
        rows_b = lax.dynamic_slice_in_dim(table_b, start_b, TILE, 0)
        relation_map = lax.dynamic_index_in_dim(relations, kinds[index], 0, keepdims=False)
        term_a, term_b, term_rel = slot_terms(rows_a, rows_b, relation_map, edges[index])
        grad_a = lax.dynamic_update_slice_in_dim(grad_a, lax.dynamic_slice_in_dim(grad_a, start_a, TILE, 0) + term_a, start_a, 0)
        grad_b = lax.dynamic_update_slice_in_dim(grad_b, lax.dynamic_slice_in_dim(grad_b, start_b, TILE, 0) + term_b, start_b, 0)
        grad_rel = grad_rel.at[kinds[index]].add(term_rel)
        return (grad_a, grad_b, grad_rel)
    start = (jnp.zeros_like(table_a), jnp.zeros_like(table_b), jnp.zeros_like(relations))
    return lax.fori_loop(jnp.int32(0), count.astype(jnp.int32), add_slot, start)

def adagrad_rows(table, state, grad):
    state_new = state + lax.optimization_barrier(jnp.mean(grad * grad, axis=1))
    table_new = table - learn_rate * grad / (jnp.sqrt(state_new)[:, None] + epsilon)
    return (table_new, state_new)

def reference(left_table, left_state, right_table, right_state, relations, relation_state, edge_weights, tile_left, tile_right, tile_relation, live_count):
    lefts_all = left_table.reshape(PARTITIONS, ROWS, D)
    left_states = left_state.reshape(PARTITIONS, ROWS)
    rights_all = right_table.reshape(PARTITIONS, ROWS, D)
    right_states = right_state.reshape(PARTITIONS, ROWS)
    rel_grad = jnp.zeros_like(relations)
    for turn in range(ROUNDS):
        visiting = jnp.roll(rights_all, turn, axis=0)
        visiting_state = jnp.roll(right_states, turn, axis=0)

        def one_holder(total, items):
            table_a, state_a, table_b, state_b, edges, lefts, rights, kinds, count = items
            grad_a, grad_b, grad_rel = bucket_grads(table_a, table_b, relations, edges, lefts, rights, kinds, count)
            table_a, state_a = adagrad_rows(table_a, state_a, grad_a)
            table_b, state_b = adagrad_rows(table_b, state_b, grad_b)
            return (total + grad_rel, (table_a, state_a, table_b, state_b))
        items = (lefts_all, left_states, visiting, visiting_state, edge_weights[:, turn], tile_left[:, turn], tile_right[:, turn], tile_relation[:, turn], live_count[:, turn])
        rel_grad, results = lax.scan(one_holder, rel_grad, items)
        lefts_all, left_states, visiting, visiting_state = results
        rights_all = jnp.roll(visiting, -turn, axis=0)
        right_states = jnp.roll(visiting_state, -turn, axis=0)
    flat_rel, flat_state = adagrad_rows(relations.reshape(RELS * D, D), relation_state.reshape(RELS * D), rel_grad.reshape(RELS * D, D))
    return (lefts_all.reshape(TABLE_ROWS, D), left_states.reshape(TABLE_ROWS), rights_all.reshape(TABLE_ROWS, D), right_states.reshape(TABLE_ROWS), flat_rel.reshape(RELS, D, D), flat_state.reshape(RELS, D))
```

```python
import functools
import jax
import jax.numpy as jnp
from jax import lax
from jax.experimental import pallas as pl
from jax.experimental.pallas import tpu as pltpu
from jax.sharding import Mesh
from jax.sharding import PartitionSpec as P

D = 256
TILE = 128
TILES = 16
ACTIVE = 16
RELS = 4
LEARN = 0.1
EPS = 1e-6
DEV = ("dev_0", "dev_1", "dev_2", "dev_3")
F32 = jnp.float32
BF16 = jnp.bfloat16


def halves(x):
    hi = x.astype(BF16)
    lo = (x - hi.astype(F32)).astype(BF16)
    return hi, lo


def product(a, b, dims):
    (ah, al), (bh, bl) = a, b
    (ca,), (cb,) = dims
    lhs = jnp.concatenate([ah, ah, al], axis=ca)
    rhs = jnp.concatenate([bh, bl, bh], axis=cb)
    return lax.dot_general(lhs, rhs, (dims, ((), ())), preferred_element_type=F32)


NN = ((1,), (0,))
NT = ((1,), (1,))


def round_kernel(
    turn,
    chained,
    lefts,
    rights,
    kinds,
    counts,
    lstate,
    rstate,
    left_in,
    right_in,
    relations,
    edges,
    *rest,
):
    if chained:
        rel_in, *rest = rest
    (
        left_out,
        lstate_out,
        right_out,
        rstate_out,
        rel_out,
        tl,
        tr,
        gl,
        gr,
        rg,
        mf,
        mh,
        ml,
        ew,
        hitl,
        hitr,
        tsem,
        esem,
        msem,
        rsem,
        osem,
    ) = rest
    count = counts[turn]
    pairs = lax.div(count + 1, 2)
    rel_load = pltpu.make_async_copy(relations, mf, msem.at[0])
    rel_load.start()
    left_load = pltpu.make_async_copy(left_in, tl, tsem.at[0])
    right_load = pltpu.make_async_copy(right_in, tr, tsem.at[1])
    left_load.start()
    right_load.start()

    def edge_copy(s):
        return pltpu.make_async_copy(edges.at[turn, s], ew.at[s], esem.at[s])

    def edge_start(s, _):
        edge_copy(s).start()
        return 0

    lax.fori_loop(0, 2 * pairs, edge_start, 0)
    if chained:
        rg_load = pltpu.make_async_copy(rel_in, rg, rsem.at[0])
        rg_load.start()
    else:
        rg[...] = jnp.zeros_like(rg)

    def clear(t, _):
        hitl[t] = 0
        hitr[t] = 0
        rows = pl.ds(t * TILE, TILE)
        gl[rows, :] = jnp.zeros((TILE, D), F32)
        gr[rows, :] = jnp.zeros((TILE, D), F32)
        return 0

    lax.fori_loop(0, TILES, clear, 0)

    def mark(s, _):
        hitl[lefts[turn, s]] = 1
        hitr[rights[turn, s]] = 1
        return 0

    lax.fori_loop(0, count, mark, 0)
    rel_load.wait()

    def split(r, _):
        hi, lo = halves(mf[r])
        mh[r] = hi
        ml[r] = lo
        return 0

    lax.fori_loop(0, RELS, split, 0)
    left_load.wait()
    right_load.wait()

    def out_copy(side, t):
        src, dst = ((tl, left_out), (tr, right_out))[side]
        rows = pl.ds(t * TILE, TILE)
        return pltpu.make_async_copy(src.at[rows, :], dst.at[rows, :], osem.at[side, t])

    def early(t, _):
        for side, hit in ((0, hitl), (1, hitr)):

            @pl.when(hit[t] == 0)
            def _():
                out_copy(side, t).start()

        return 0

    lax.fori_loop(0, TILES, early, 0)
    if chained:
        rg_load.wait()

    def pair(i, _):
        slots = (2 * i, 2 * i + 1)
        for s in slots:
            edge_copy(s).wait()
        at = [lefts[turn, s] * TILE for s in slots]
        bt = [rights[turn, s] * TILE for s in slots]
        kd = [kinds[turn, s] for s in slots]
        live = [jnp.where(s < count, 1.0, 0.0).astype(F32) for s in slots]
        af = [tl[pl.ds(a, TILE), :] for a in at]
        a = [halves(x) for x in af]
        m = [(mh[k], ml[k]) for k in kd]
        p = [halves(product(x, y, NN)) for x, y in zip(a, m)]
        b = [halves(tr[pl.ds(x, TILE), :]) for x in bt]
        s_ = [product(x, y, NT) for x, y in zip(p, b)]
        g = []
        for s, sc, lv in zip(slots, s_, live):
            w = ew[s]
            zero = w == 0
            sc = sc * (D**-0.5)
            sig = jax.nn.sigmoid(jnp.where(zero, sc, -sc))
            coef = jnp.where(zero, 1.0, w.astype(F32) * (-1.0 / 3.0))
            g.append(sig * coef * (lv * D**-0.5))
        gs = [halves(x) for x in g]
        gts = [halves(x.T) for x in g]
        backed = [halves(product(x, y, NN)) for x, y in zip(gs, b)]
        tb = [product(x, y, NN) for x, y in zip(gts, p)]
        ta = [product(x, y, NT) for x, y in zip(backed, m)]
        ats = [halves(x.T) for x in af]
        tm = [product(x, y, NN) for x, y in zip(ats, backed)]
        for j in range(2):
            rows = pl.ds(bt[j], TILE)
            gr[rows, :] += tb[j]
        for j in range(2):
            rows = pl.ds(at[j], TILE)
            gl[rows, :] += ta[j]
        for j in range(2):
            rg[kd[j]] += tm[j]
        return 0

    lax.fori_loop(0, pairs, pair, 0)
    rg_store = pltpu.make_async_copy(rg, rel_out, rsem.at[1])
    rg_store.start()
    lstate_out[...] = lstate[...]
    rstate_out[...] = rstate[...]

    def update(side, t):
        tab, grad, st, st_out = ((tl, gl, lstate, lstate_out), (tr, gr, rstate, rstate_out))[side]
        rows = pl.ds(t * TILE, TILE)
        g = grad[rows, :]
        mean = jnp.sum(g * g, axis=1, keepdims=True) * (1.0 / D)
        row = st[pl.ds(t, 1), :]
        wide = jnp.broadcast_to(row, (TILE, TILE)).T + mean
        st_out[pl.ds(t, 1), :] = wide.T[0:1, :]
        step = LEARN / (jnp.sqrt(wide) + EPS)
        tab[rows, :] = tab[rows, :] - g * jnp.concatenate([step, step], axis=1)

    def finish(t, _):
        before = jnp.maximum(t - 1, 0)
        for side, hit in ((0, hitl), (1, hitr)):

            @pl.when((t < TILES) & (hit[jnp.minimum(t, TILES - 1)] != 0))
            def _():
                update(side, t)

            @pl.when((t > 0) & (hit[before] != 0))
            def _():
                out_copy(side, before).start()

        return 0

    lax.fori_loop(0, TILES + 1, finish, 0)

    def drain(t, _):
        out_copy(0, t).wait()
        out_copy(1, t).wait()
        return 0

    lax.fori_loop(0, TILES, drain, 0)
    rg_store.wait()


def run_round(turn, ids, left, lstate, right, rstate, relations, edges, rel_grad):
    smem = pl.BlockSpec(memory_space=pltpu.SMEM)
    vmem = pl.BlockSpec(memory_space=pltpu.VMEM)
    hbm = pl.BlockSpec(memory_space=pl.ANY)
    rows = TILES * TILE
    args = (*ids, lstate, rstate, left, right, relations, edges)
    specs = [smem] * 4 + [vmem] * 2 + [hbm] * 4
    if rel_grad is not None:
        args += (rel_grad,)
        specs += [hbm]
    return pl.pallas_call(
        functools.partial(round_kernel, turn, rel_grad is not None),
        name="bucket_round",
        out_shape=(
            jax.ShapeDtypeStruct((rows, D), F32),
            jax.ShapeDtypeStruct((TILES, TILE), F32),
            jax.ShapeDtypeStruct((rows, D), F32),
            jax.ShapeDtypeStruct((TILES, TILE), F32),
            jax.ShapeDtypeStruct((RELS, D, D), F32),
        ),
        in_specs=specs,
        out_specs=(hbm, vmem, hbm, vmem, hbm),
        scratch_shapes=[
            pltpu.VMEM((rows, D), F32),
            pltpu.VMEM((rows, D), F32),
            pltpu.VMEM((rows, D), F32),
            pltpu.VMEM((rows, D), F32),
            pltpu.VMEM((RELS, D, D), F32),
            pltpu.VMEM((RELS, D, D), F32),
            pltpu.VMEM((RELS, D, D), BF16),
            pltpu.VMEM((RELS, D, D), BF16),
            pltpu.VMEM((ACTIVE, TILE, TILE), jnp.int32),
            pltpu.SMEM((TILES,), jnp.int32),
            pltpu.SMEM((TILES,), jnp.int32),
            pltpu.SemaphoreType.DMA((2,)),
            pltpu.SemaphoreType.DMA((ACTIVE,)),
            pltpu.SemaphoreType.DMA((1,)),
            pltpu.SemaphoreType.DMA((2,)),
            pltpu.SemaphoreType.DMA((2, TILES)),
        ],
        compiler_params=pltpu.CompilerParams(vmem_limit_bytes=62 << 20),
        cost_estimate=pl.CostEstimate(
            flops=2_400_000_000, bytes_accessed=12_000_000, transcendentals=262144
        ),
    )(*args)


AXES = (("dev_0", 8), ("dev_1", 4), ("dev_2", 4), ("dev_3", 2))
FIRST = 6 * 128
MESH = pl.DeviceIdType.MESH


def coordinates(index):
    z = lax.rem(lax.div(index, 32), 8)
    y = lax.rem(lax.div(index, 8), 4)
    x = lax.rem(lax.div(index, 2), 4)
    return (z, y, x, lax.rem(index, 2))


def home_kernel(
    back_left,
    back_right,
    left,
    lstate,
    right,
    rstate,
    grad,
    rel,
    rel_state,
    left_out,
    lstate_out,
    right_out,
    rstate_out,
    rel_out,
    rel_state_out,
    cbuf,
    yacc,
    ybuf,
    zacc,
    zbuf,
    xbuf,
    full,
    home_send,
    home_recv,
    csend,
    crecv,
    ysend,
    yrecv,
    zsend,
    zrecv,
    xsend,
    xrecv,
):
    z, y, x, c = (lax.axis_index(name) for name, _ in AXES)
    me = ((z * 4 + y) * 4 + x) * 2 + c
    count = 256

    def shifted_id(distance):
        return coordinates(lax.rem(me + count + distance, count))

    far = [(lax.rem(z + d, 8), y, x, c) for d in range(1, 8)]
    side = [(z, lax.rem(y + d, 4), x, c) for d in range(1, 4)]
    row = [(z, y, lax.rem(x + d, 4), c) for d in range(1, 4)]
    mate = (z, y, x, 1 - c)
    lines = [shifted_id(d) for d in (back_left, -back_left, back_right, -back_right)]
    peers = lines + [mate] + far + side + row
    barrier = pltpu.get_barrier_semaphore()
    for peer in peers:
        pl.semaphore_signal(barrier, inc=1, device_id=peer, device_id_type=MESH)
    pl.semaphore_wait(barrier, len(peers))

    def send(src, dst, ssem, rsem, peer):
        copy = pltpu.make_async_remote_copy(
            src_ref=src,
            dst_ref=dst,
            send_sem=ssem,
            recv_sem=rsem,
            device_id=peer,
            device_id_type=MESH,
        )
        copy.start()
        return copy

    half = 512
    copies = [
        send(
            grad.at[pl.ds((1 - c) * half, half), :], cbuf, csend.at[0], crecv.at[0], mate
        )
    ]
    homes = [
        send(rstate, rstate_out, home_send.at[0], home_recv.at[0], lines[2]),
        send(lstate, lstate_out, home_send.at[1], home_recv.at[1], lines[0]),
    ]

    def send_home(part, start, length):
        rows = pl.ds(start, length)
        for i, (src, dst, peer) in enumerate(
            ((right, right_out, lines[2]), (left, left_out, lines[0]))
        ):
            at = 2 + 2 * part + i
            homes.append(
                send(src.at[rows, :], dst.at[rows, :], home_send.at[at], home_recv.at[at], peer)
            )

    copies[0].wait()

    def add_core(i, _):
        rows = pl.ds(i * TILE, TILE)
        yacc[i] = grad[pl.ds(c * half + i * TILE, TILE), :] + cbuf[rows, :]
        return 0

    lax.fori_loop(0, 4, add_core, 0)
    copies = [
        send(yacc.at[peer[1]], ybuf.at[d], ysend.at[d], yrecv.at[d], peer)
        for d, peer in enumerate(side)
    ]
    send_home(0, 0, FIRST)
    for copy in copies:
        copy.wait()

    def add_side(i, _):
        rows = pl.ds(i * 16, 16)
        zacc[i] = (yacc[y, rows, :] + ybuf[0, rows, :]) + (ybuf[1, rows, :] + ybuf[2, rows, :])
        return 0

    lax.fori_loop(0, 8, add_side, 0)
    copies = [
        send(zacc.at[peer[0]], zbuf.at[d], zsend.at[d], zrecv.at[d], peer)
        for d, peer in enumerate(far)
    ]
    for copy in copies:
        copy.wait()
    own = zacc[z]
    for d in range(7):
        own = own + zbuf[d]
    xbuf[x] = own
    copies = [
        send(xbuf.at[x], xbuf.at[x], xsend.at[d], xrecv.at[d], peer) for d, peer in enumerate(row)
    ]
    for copy in copies:
        copy.wait()
    full[c, y, z] = (xbuf[0] + xbuf[1]) + (xbuf[2] + xbuf[3])
    piece = full.at[c, y, z]
    copies = [
        send(piece, piece, zsend.at[7 + d], zrecv.at[7 + d], peer) for d, peer in enumerate(far)
    ]
    for copy in copies:
        copy.wait()
    piece = full.at[c, y]
    copies = [
        send(piece, piece, ysend.at[3 + d], yrecv.at[3 + d], peer) for d, peer in enumerate(side)
    ]
    send_home(1, FIRST, left.shape[0] - FIRST)
    for copy in copies:
        copy.wait()
    piece = full.at[c]
    send(piece, piece, csend.at[1], crecv.at[1], mate).wait()

    def update(t, _):
        rows = pl.ds(t * TILE, TILE)
        g = full[lax.div(t, 4), lax.rem(t, 4)].reshape(TILE, D)
        mean = jnp.sum(g * g, axis=1, keepdims=True) * (1.0 / D)
        wide = jnp.broadcast_to(rel_state[pl.ds(t, 1), :], (TILE, TILE)).T + mean
        rel_state_out[pl.ds(t, 1), :] = wide.T[0:1, :]
        step = LEARN / (jnp.sqrt(wide) + EPS)
        rel_out[rows, :] = rel[rows, :] - g * jnp.concatenate([step, step], axis=1)
        return 0

    lax.fori_loop(0, 8, update, 0)
    for copy in homes:
        copy.wait()


def bring_home(back_left, back_right, left, lstate, right, rstate, grad, rel, rel_state):
    vmem = pl.BlockSpec(memory_space=pltpu.VMEM)
    hbm = pl.BlockSpec(memory_space=pl.ANY)
    like = lambda a: jax.ShapeDtypeStruct(a.shape, a.dtype)
    dma = pltpu.SemaphoreType.DMA
    return pl.pallas_call(
        functools.partial(home_kernel, back_left, back_right),
        name="bring_home",
        out_shape=tuple(like(a) for a in (left, lstate, right, rstate, rel, rel_state)),
        in_specs=[hbm] * 4 + [vmem] * 3,
        out_specs=(hbm,) * 4 + (vmem,) * 2,
        scratch_shapes=[
            pltpu.VMEM((512, D), F32),
            pltpu.VMEM((4, TILE, D), F32),
            pltpu.VMEM((3, TILE, D), F32),
            pltpu.VMEM((8, 16, D), F32),
            pltpu.VMEM((7, 16, D), F32),
            pltpu.VMEM((4, 16, D), F32),
            pltpu.VMEM((2, 4, 8, 16, D), F32),
            dma((6,)),
            dma((6,)),
            dma((2,)),
            dma((2,)),
            dma((6,)),
            dma((6,)),
            dma((14,)),
            dma((14,)),
            dma((3,)),
            dma((3,)),
        ],
        compiler_params=pltpu.CompilerParams(
            collective_id=0, has_side_effects=True, vmem_limit_bytes=62 << 20
        ),
        cost_estimate=pl.CostEstimate(
            flops=2_000_000, bytes_accessed=12_000_000, transcendentals=1024
        ),
    )(left, lstate, right, rstate, grad, rel, rel_state)


def shifted(block, axis, distance):
    devices = range(lax.axis_size(axis))
    route = [((i - distance) % len(devices), i) for i in devices]
    return lax.ppermute(block, axis, route)


def per_device(
    left_table,
    left_state,
    right_table,
    right_state,
    relations,
    relation_state,
    edge_weights,
    tile_left,
    tile_right,
    tile_relation,
    live_count,
):
    edges = edge_weights[0]
    ids = (tile_left[0], tile_right[0], tile_relation[0], live_count[0])
    rounds = edges.shape[0]
    last = rounds - 1
    packed = jnp.concatenate([x[last].reshape(-1) for x in ids])
    last_edges, packed = shifted((edges[last:], packed), DEV, -1)
    rel_grad = None
    table_left, state_left = left_table, left_state.reshape(TILES, TILE)
    table_right, state_right = right_table, right_state.reshape(TILES, TILE)
    for turn in range(last):
        table_left, state_left, table_right, state_right, rel_grad = run_round(
            turn, ids, table_left, state_left, table_right, state_right, relations, edges, rel_grad
        )
        if turn + 1 < last:
            table_right, state_right = shifted((table_right, state_right), DEV, 1)
        if turn == 0:
            table_right, last_edges, packed = lax.optimization_barrier(
                (table_right, last_edges, packed)
            )
    last_ids = [packed[i * ACTIVE : (i + 1) * ACTIVE].reshape(1, ACTIVE) for i in range(3)]
    last_ids.append(packed[3 * ACTIVE :])
    table_left, state_left = shifted((table_left, state_left), DEV, -1)
    table_left, state_left, table_right, state_right, rel_grad = run_round(
        0, last_ids, table_left, state_left, table_right, state_right, relations, last_edges, rel_grad
    )
    kinds_count, width = (relations.shape[0], relations.shape[1])
    table_left, state_left, table_right, state_right, new_rel, new_state = bring_home(
        1,
        1 - last,
        table_left,
        state_left,
        table_right,
        state_right,
        rel_grad.reshape(kinds_count * width, width),
        relations.reshape(kinds_count * width, width),
        relation_state.reshape(-1, TILE),
    )
    return (
        table_left,
        state_left.reshape(-1),
        table_right,
        state_right.reshape(-1),
        new_rel.reshape(kinds_count, width, width),
        new_state.reshape(kinds_count, width),
    )


def solution(mesh):
    torus = Mesh(mesh.devices.reshape(8, 4, 4, 2), ("dev_0", "dev_1", "dev_2", "dev_3"))
    return jax.shard_map(
        per_device,
        mesh=torus,
        in_specs=(
            P(DEV, None),
            P(DEV),
            P(DEV, None),
            P(DEV),
            P(),
            P(),
            P(DEV, None, None, None, None),
            P(DEV, None, None),
            P(DEV, None, None),
            P(DEV, None, None),
            P(DEV, None),
        ),
        out_specs=(P(DEV, None), P(DEV), P(DEV, None), P(DEV), P(), P()),
        check_vma=False,
    )
```

```python
import functools
import jax
import jax.numpy as jnp
from jax import lax
from jax.experimental import pallas as pl
from jax.experimental.pallas import tpu as pltpu
from jax.sharding import Mesh
from jax.sharding import PartitionSpec as P

D = 256
TILE = 128
TILES = 16
ACTIVE = 16
RELS = 4
LEARN = 0.1
EPS = 1e-6
DEV = ("dev_0", "dev_1", "dev_2", "dev_3")
F32 = jnp.float32
BF16 = jnp.bfloat16


def halves(x):
    hi = x.astype(BF16)
    lo = (x - hi.astype(F32)).astype(BF16)
    return hi, lo


def product(a, b, dims):
    (ah, al), (bh, bl) = a, b
    (ca,), (cb,) = dims
    rows, depth = ah.shape
    if depth == TILE:
        lhs = jnp.concatenate([ah, al, ah], axis=ca)
        rhs = jnp.concatenate([bh, bh, bl], axis=cb)
        return lax.dot_general(lhs, rhs, (dims, ((), ())), preferred_element_type=F32)
    dot = functools.partial(
        lax.dot_general, dimension_numbers=(dims, ((), ())), preferred_element_type=F32
    )
    both = dot(jnp.concatenate([ah, al], axis=0), bh)
    return (both[:rows] + both[rows:]) + dot(ah, bl)


NN = ((1,), (0,))
NT = ((1,), (1,))


def round_kernel(
    turn,
    chained,
    in_place,
    lefts,
    rights,
    kinds,
    counts,
    lstate,
    rstate,
    left_in,
    right_in,
    relations,
    edges,
    *rest,
):
    if chained:
        rel_in, *rest = rest
    (
        left_out,
        lstate_out,
        right_out,
        rstate_out,
        rel_out,
        tl,
        tr,
        gl,
        gr,
        rg,
        mf,
        mh,
        ml,
        ew,
        stl,
        str_,
        hit,
        order,
        num,
        tsem,
        esem,
        msem,
        rsem,
        osem,
    ) = rest
    count = counts[turn]
    pairs = lax.div(count + 1, 2)
    tables = ((tl, left_in, left_out, lefts, gl), (tr, right_in, right_out, rights, gr))

    def tile_load(side, t):
        table, src, *_ = tables[side]
        rows = pl.ds(t * TILE, TILE)
        return pltpu.make_async_copy(src.at[rows, :], table.at[rows, :], tsem.at[side, t])

    def tile_store(side, t):
        table, _, dst, *_ = tables[side]
        rows = pl.ds(t * TILE, TILE)
        return pltpu.make_async_copy(table.at[rows, :], dst.at[rows, :], osem.at[side, t])

    def edge_copy(s):
        return pltpu.make_async_copy(edges.at[turn, s], ew.at[s], esem.at[s])

    rel_load = pltpu.make_async_copy(relations, mf, msem.at[0])
    rel_load.start()
    for side in range(2):
        num[side] = 0
        for t in range(TILES):
            hit[side, t] = 0
            order[side, t] = TILES

    def mark(s, _):
        edge_copy(s).start()
        for side in range(2):
            t = tables[side][3][turn, s]

            @pl.when(hit[side, t] == 0)
            def _():
                tile_load(side, t).start()
                hit[side, t] = 1
                order[side, num[side]] = t
                num[side] = num[side] + 1

        return 0

    lax.fori_loop(0, 2 * pairs, mark, 0)
    if chained:
        rg_load = pltpu.make_async_copy(rel_in, rg, rsem.at[0])
        rg_load.start()
    else:
        rg[...] = jnp.zeros_like(rg)

    def each_hit(side, act):
        def body(i, _):
            act(order[side, i])
            return 0

        lax.fori_loop(0, num[side], body, 0)

    def each_other(act):
        def body(t, _):
            for side in range(2):

                @pl.when(hit[side, t] == 0)
                def _():
                    act(side, t)

            return 0

        lax.fori_loop(0, TILES, body, 0)

    if not in_place:
        each_other(lambda side, t: tile_load(side, t).start())
    for side, (table, _, _, _, grad) in enumerate(tables):

        def clear(t):
            grad[pl.ds(t * TILE, TILE), :] = jnp.zeros((TILE, D), F32)

        each_hit(side, clear)
        spare = pl.ds(TILES * TILE, TILE)
        grad[spare, :] = jnp.zeros((TILE, D), F32)
        table[spare, :] = jnp.zeros((TILE, D), F32)
    for st, old in ((stl, lstate), (str_, rstate)):
        st[pl.ds(0, TILES), :] = old[...]
        st[pl.ds(TILES, 8), :] = jnp.zeros((8, TILE), F32)
    rel_load.wait()

    def split(r, _):
        hi, lo = halves(mf[r])
        mh[r] = hi
        ml[r] = lo
        return 0

    lax.fori_loop(0, RELS, split, 0)
    for side in range(2):
        each_hit(side, lambda t: tile_load(side, t).wait())
    if chained:
        rg_load.wait()

    def pair(i, _):
        slots = (2 * i, 2 * i + 1)
        for s in slots:
            edge_copy(s).wait()
        at = [lefts[turn, s] * TILE for s in slots]
        bt = [rights[turn, s] * TILE for s in slots]
        kd = [kinds[turn, s] for s in slots]
        live = [jnp.where(s < count, 1.0, 0.0).astype(F32) for s in slots]
        af = [tl[pl.ds(a, TILE), :] for a in at]
        a = [halves(x) for x in af]
        m = [(mh[k], ml[k]) for k in kd]
        p = [halves(product(x, y, NN)) for x, y in zip(a, m)]
        b = [halves(tr[pl.ds(x, TILE), :]) for x in bt]
        s_ = [product(x, y, NT) for x, y in zip(p, b)]
        g = []
        for s, sc, lv in zip(slots, s_, live):
            w = ew[s]
            zero = w == 0
            sc = sc * (D**-0.5)
            sig = jax.nn.sigmoid(jnp.where(zero, sc, -sc))
            coef = jnp.where(zero, 1.0, w.astype(F32) * (-1.0 / 3.0))
            g.append(sig * coef * (lv * D**-0.5))
        gs = [halves(x) for x in g]
        gts = [halves(x.T) for x in g]
        backed = [halves(product(x, y, NN)) for x, y in zip(gs, b)]
        tb = [product(x, y, NN) for x, y in zip(gts, p)]
        ta = [product(x, y, NT) for x, y in zip(backed, m)]
        ats = [halves(x.T) for x in af]
        tm = [product(x, y, NN) for x, y in zip(ats, backed)]
        for j in range(2):
            rows = pl.ds(bt[j], TILE)
            gr[rows, :] += tb[j]
        for j in range(2):
            rows = pl.ds(at[j], TILE)
            gl[rows, :] += ta[j]
        for j in range(2):
            rg[kd[j]] += tm[j]
        return 0

    lax.fori_loop(0, pairs, pair, 0)
    rg_store = pltpu.make_async_copy(rg, rel_out, rsem.at[1])
    rg_store.start()
    if not in_place:

        def pass_on(side, t):
            tile_load(side, t).wait()
            tile_store(side, t).start()

        each_other(pass_on)
    steps = jnp.maximum(num[0], num[1])

    def update(table, grad, st, t):
        rows = pl.ds(t * TILE, TILE)
        g = grad[rows, :]
        mean = jnp.sum(g * g, axis=1, keepdims=True) * (1.0 / D)
        wide = jnp.broadcast_to(st[pl.ds(t, 1), :], (TILE, TILE)).T + mean
        step = LEARN / (jnp.sqrt(wide) + EPS)
        new = table[rows, :] - g * jnp.concatenate([step, step], axis=1)
        return rows, new, wide.T[0:1, :]

    def finish(i, _):
        @pl.when(i < steps)
        def _():
            both = ((tl, gl, stl), (tr, gr, str_))
            at = [order[side, i] for side in range(2)]
            out = [update(*refs, t) for refs, t in zip(both, at)]
            for (table, _, st), t, (rows, new, line) in zip(both, at, out):
                table[rows, :] = new
                st[pl.ds(t, 1), :] = line

        before = jnp.maximum(i - 1, 0)
        for side in range(2):

            @pl.when((i > 0) & (before < num[side]))
            def _():
                tile_store(side, order[side, before]).start()

        return 0

    lax.fori_loop(0, steps + 1, finish, 0)
    lstate_out[...] = stl[pl.ds(0, TILES), :]
    rstate_out[...] = str_[pl.ds(0, TILES), :]
    for side in range(2):
        each_hit(side, lambda t: tile_store(side, t).wait())
    if not in_place:
        each_other(lambda side, t: tile_store(side, t).wait())
    rg_store.wait()


def run_round(turn, ids, left, lstate, right, rstate, relations, edges, rel_grad):
    smem = pl.BlockSpec(memory_space=pltpu.SMEM)
    vmem = pl.BlockSpec(memory_space=pltpu.VMEM)
    hbm = pl.BlockSpec(memory_space=pl.ANY)
    rows = TILES * TILE
    args = (*ids, lstate, rstate, left, right, relations, edges)
    specs = [smem] * 4 + [vmem] * 2 + [hbm] * 4
    chained = rel_grad is not None
    if chained:
        args += (rel_grad,)
        specs += [hbm]
    return pl.pallas_call(
        functools.partial(round_kernel, turn, chained, chained),
        name="bucket_round",
        out_shape=(
            jax.ShapeDtypeStruct((rows, D), F32),
            jax.ShapeDtypeStruct((TILES, TILE), F32),
            jax.ShapeDtypeStruct((rows, D), F32),
            jax.ShapeDtypeStruct((TILES, TILE), F32),
            jax.ShapeDtypeStruct((RELS, D, D), F32),
        ),
        in_specs=specs,
        out_specs=(hbm, vmem, hbm, vmem, hbm),
        scratch_shapes=[
            pltpu.VMEM((rows + TILE, D), F32),
            pltpu.VMEM((rows + TILE, D), F32),
            pltpu.VMEM((rows + TILE, D), F32),
            pltpu.VMEM((rows + TILE, D), F32),
            pltpu.VMEM((RELS, D, D), F32),
            pltpu.VMEM((RELS, D, D), F32),
            pltpu.VMEM((RELS, D, D), BF16),
            pltpu.VMEM((RELS, D, D), BF16),
            pltpu.VMEM((ACTIVE, TILE, TILE), jnp.int32),
            pltpu.VMEM((TILES + 8, TILE), F32),
            pltpu.VMEM((TILES + 8, TILE), F32),
            pltpu.SMEM((2, TILES), jnp.int32),
            pltpu.SMEM((2, TILES), jnp.int32),
            pltpu.SMEM((2,), jnp.int32),
            pltpu.SemaphoreType.DMA((2, TILES)),
            pltpu.SemaphoreType.DMA((ACTIVE,)),
            pltpu.SemaphoreType.DMA((1,)),
            pltpu.SemaphoreType.DMA((2,)),
            pltpu.SemaphoreType.DMA((2, TILES)),
        ],
        input_output_aliases={6: 0, 7: 2} if chained else {},
        compiler_params=pltpu.CompilerParams(vmem_limit_bytes=62 << 20),
        cost_estimate=pl.CostEstimate(
            flops=2_400_000_000, bytes_accessed=12_000_000, transcendentals=262144
        ),
    )(*args)


AXES = (("dev_0", 8), ("dev_1", 4), ("dev_2", 4), ("dev_3", 2))
PARTS = (6, 3, 2, 3, 2)
MESH = pl.DeviceIdType.MESH


def coordinates(index):
    z = lax.rem(lax.div(index, 32), 8)
    y = lax.rem(lax.div(index, 8), 4)
    x = lax.rem(lax.div(index, 2), 4)
    return (z, y, x, lax.rem(index, 2))


def home_kernel(
    back_left,
    back_right,
    left,
    lstate,
    right,
    rstate,
    grad,
    rel,
    rel_state,
    left_out,
    lstate_out,
    right_out,
    rstate_out,
    rel_out,
    rel_state_out,
    cbuf,
    xacc,
    xbuf,
    zacc,
    zbuf,
    ybuf,
    full,
    home_send,
    home_recv,
    csend,
    crecv,
    ysend,
    yrecv,
    zsend,
    zrecv,
    xsend,
    xrecv,
):
    z, y, x, c = (lax.axis_index(name) for name, _ in AXES)
    me = ((z * 4 + y) * 4 + x) * 2 + c
    count = 256

    def shifted_id(distance):
        return coordinates(lax.rem(me + count + distance, count))

    far = [(lax.rem(z + d, 8), y, x, c) for d in range(1, 8)]
    side = [(z, y, lax.rem(x + d, 4), c) for d in range(1, 4)]
    row = [(z, lax.rem(y + d, 4), x, c) for d in range(1, 4)]
    mate = (z, y, x, 1 - c)
    lines = [shifted_id(d) for d in (back_left, -back_left, back_right, -back_right)]
    peers = lines + [mate] + far + side + row
    barrier = pltpu.get_barrier_semaphore()
    for peer in peers:
        pl.semaphore_signal(barrier, inc=1, device_id=peer, device_id_type=MESH)
    pl.semaphore_wait(barrier, len(peers))

    def send(src, dst, ssem, rsem, peer):
        copy = pltpu.make_async_remote_copy(
            src_ref=src,
            dst_ref=dst,
            send_sem=ssem,
            recv_sem=rsem,
            device_id=peer,
            device_id_type=MESH,
        )
        copy.start()
        return copy

    half = 512
    copies = [
        send(
            grad.at[pl.ds((1 - c) * half, half), :], cbuf, csend.at[0], crecv.at[0], mate
        )
    ]
    homes = [
        send(rstate, rstate_out, home_send.at[0], home_recv.at[0], lines[2]),
        send(lstate, lstate_out, home_send.at[1], home_recv.at[1], lines[0]),
    ]

    def send_home(part):
        rows = pl.ds(sum(PARTS[:part]) * TILE, PARTS[part] * TILE)
        for i, (src, dst, peer) in enumerate(
            ((right, right_out, lines[2]), (left, left_out, lines[0]))
        ):
            at = 2 + 2 * part + i
            homes.append(
                send(src.at[rows, :], dst.at[rows, :], home_send.at[at], home_recv.at[at], peer)
            )

    copies[0].wait()

    def add_core(i, _):
        rows = pl.ds(i * TILE, TILE)
        part = pl.ds(lax.rem(i, 2) * TILE, TILE)
        xacc[lax.div(i, 2), part, :] = grad[pl.ds(c * half + i * TILE, TILE), :] + cbuf[rows, :]
        return 0

    lax.fori_loop(0, 4, add_core, 0)
    inner = (x == 1) | (x == 2)
    mine = lax.rem(x + 3, 4)

    def described(src, dst, ssem, rsem, peer):
        return pltpu.make_async_remote_copy(
            src_ref=src,
            dst_ref=dst,
            send_sem=ssem,
            recv_sem=rsem,
            device_id=peer,
            device_id_type=MESH,
        )

    def to_column(j):
        slot = lax.rem(x - j + 2, 4)
        return described(
            xacc.at[j], xbuf.at[slot], xsend.at[j], xrecv.at[slot], (z, y, 1 + j, c)
        )

    def from_row(slot):
        return described(xbuf.at[slot], xbuf.at[slot], xsend.at[0], xrecv.at[slot], side[0])

    for j in range(2):

        @pl.when(x != 1 + j)
        def _():
            to_column(j).start()

    send_home(0)
    for j in range(2):

        @pl.when(x != 1 + j)
        def _():
            to_column(j).wait_send()

    @pl.when(inner)
    def _():
        for slot in range(3):
            from_row(slot).wait_recv()

        def add_row(i, _):
            rows = pl.ds(i * 32, 32)
            zacc[i] = (xacc[mine, rows, :] + xbuf[0, rows, :]) + (
                xbuf[1, rows, :] + xbuf[2, rows, :]
            )
            return 0

        lax.fori_loop(0, 8, add_row, 0)
        for d, peer in enumerate(far):
            described(zacc.at[peer[0]], zbuf.at[d], zsend.at[d], zrecv.at[d], peer).start()

    send_home(1)

    @pl.when(inner)
    def _():
        for d, peer in enumerate(far):
            described(zacc.at[peer[0]], zbuf.at[d], zsend.at[d], zrecv.at[d], peer).wait()
        own = zacc[z]
        for d in range(7):
            own = own + zbuf[d]
        ybuf[y] = own
        for d, peer in enumerate(row):
            described(ybuf.at[y], ybuf.at[y], ysend.at[d], yrecv.at[d], peer).start()

    send_home(2)

    @pl.when(inner)
    def _():
        for d, peer in enumerate(row):
            described(ybuf.at[y], ybuf.at[y], ysend.at[d], yrecv.at[d], peer).wait()
        full[c, mine, z] = (ybuf[0] + ybuf[1]) + (ybuf[2] + ybuf[3])
        piece = full.at[c, mine, z]
        for d, peer in enumerate(far):
            described(piece, piece, zsend.at[7 + d], zrecv.at[7 + d], peer).start()

    send_home(3)

    def spread(j, d):
        piece = full.at[c, j]
        slot = 3 * j + d
        return described(piece, piece, xsend.at[2 + d], xrecv.at[3 + slot], (z, y, lax.rem(x + 1 + d, 4), c))

    @pl.when(inner)
    def _():
        piece = full.at[c, mine, z]
        for d, peer in enumerate(far):
            described(piece, piece, zsend.at[7 + d], zrecv.at[7 + d], peer).wait()
        for d in range(3):
            spread(mine, d).start()

    send_home(4)

    @pl.when(inner)
    def _():
        for d in range(3):
            spread(mine, d).wait_send()

    for j in range(2):

        @pl.when(x != 1 + j)
        def _():
            spread(j, lax.rem(x - j + 2, 4)).wait_recv()

    piece = full.at[c]
    send(piece, piece, csend.at[1], crecv.at[1], mate).wait()

    def update(t, _):
        rows = pl.ds(t * TILE, TILE)
        part = pl.ds(lax.rem(t, 2) * 4, 4)
        g = full[lax.div(t, 4), lax.rem(lax.div(t, 2), 2), part].reshape(TILE, D)
        mean = jnp.sum(g * g, axis=1, keepdims=True) * (1.0 / D)
        wide = jnp.broadcast_to(rel_state[pl.ds(t, 1), :], (TILE, TILE)).T + mean
        rel_state_out[pl.ds(t, 1), :] = wide.T[0:1, :]
        step = LEARN / (jnp.sqrt(wide) + EPS)
        rel_out[rows, :] = rel[rows, :] - g * jnp.concatenate([step, step], axis=1)
        return 0

    lax.fori_loop(0, 8, update, 0)
    for copy in homes:
        copy.wait()


def bring_home(back_left, back_right, left, lstate, right, rstate, grad, rel, rel_state):
    vmem = pl.BlockSpec(memory_space=pltpu.VMEM)
    hbm = pl.BlockSpec(memory_space=pl.ANY)
    like = lambda a: jax.ShapeDtypeStruct(a.shape, a.dtype)
    dma = pltpu.SemaphoreType.DMA
    return pl.pallas_call(
        functools.partial(home_kernel, back_left, back_right),
        name="bring_home",
        out_shape=tuple(like(a) for a in (left, lstate, right, rstate, rel, rel_state)),
        in_specs=[hbm] * 4 + [vmem] * 3,
        out_specs=(hbm,) * 4 + (vmem,) * 2,
        scratch_shapes=[
            pltpu.VMEM((512, D), F32),
            pltpu.VMEM((2, 256, D), F32),
            pltpu.VMEM((3, 256, D), F32),
            pltpu.VMEM((8, 32, D), F32),
            pltpu.VMEM((7, 32, D), F32),
            pltpu.VMEM((4, 32, D), F32),
            pltpu.VMEM((2, 2, 8, 32, D), F32),
            dma((12,)),
            dma((12,)),
            dma((2,)),
            dma((2,)),
            dma((3,)),
            dma((3,)),
            dma((14,)),
            dma((14,)),
            dma((5,)),
            dma((9,)),
        ],
        compiler_params=pltpu.CompilerParams(
            collective_id=0, has_side_effects=True, vmem_limit_bytes=62 << 20
        ),
        cost_estimate=pl.CostEstimate(
            flops=2_000_000, bytes_accessed=12_000_000, transcendentals=1024
        ),
    )(left, lstate, right, rstate, grad, rel, rel_state)


def shifted(block, axis, distance):
    devices = range(lax.axis_size(axis))
    route = [((i - distance) % len(devices), i) for i in devices]
    return lax.ppermute(block, axis, route)


def per_device(
    left_table,
    left_state,
    right_table,
    right_state,
    relations,
    relation_state,
    edge_weights,
    tile_left,
    tile_right,
    tile_relation,
    live_count,
):
    edges = edge_weights[0]
    ids = (tile_left[0], tile_right[0], tile_relation[0], live_count[0])
    rounds = edges.shape[0]
    last = rounds - 1
    packed = jnp.concatenate([x[last].reshape(-1) for x in ids])
    last_edges, packed = shifted((edges[last:], packed), DEV, -1)
    rel_grad = None
    table_left, state_left = left_table, left_state.reshape(TILES, TILE)
    table_right, state_right = right_table, right_state.reshape(TILES, TILE)
    for turn in range(last):
        table_left, state_left, table_right, state_right, rel_grad = run_round(
            turn, ids, table_left, state_left, table_right, state_right, relations, edges, rel_grad
        )
        if turn + 1 < last:
            table_right, state_right = shifted((table_right, state_right), DEV, 1)
        if turn == 0:
            table_right, last_edges, packed = lax.optimization_barrier(
                (table_right, last_edges, packed)
            )
    last_ids = [packed[i * ACTIVE : (i + 1) * ACTIVE].reshape(1, ACTIVE) for i in range(3)]
    last_ids.append(packed[3 * ACTIVE :])
    table_left, state_left = shifted((table_left, state_left), DEV, -1)
    table_left, state_left, table_right, state_right, rel_grad = run_round(
        0, last_ids, table_left, state_left, table_right, state_right, relations, last_edges, rel_grad
    )
    kinds_count, width = (relations.shape[0], relations.shape[1])
    table_left, state_left, table_right, state_right, new_rel, new_state = bring_home(
        1,
        1 - last,
        table_left,
        state_left,
        table_right,
        state_right,
        rel_grad.reshape(kinds_count * width, width),
        relations.reshape(kinds_count * width, width),
        relation_state.reshape(-1, TILE),
    )
    return (
        table_left,
        state_left.reshape(-1),
        table_right,
        state_right.reshape(-1),
        new_rel.reshape(kinds_count, width, width),
        new_state.reshape(kinds_count, width),
    )


def solution(mesh):
    torus = Mesh(mesh.devices.reshape(8, 4, 4, 2), ("dev_0", "dev_1", "dev_2", "dev_3"))
    return jax.shard_map(
        per_device,
        mesh=torus,
        in_specs=(
            P(DEV, None),
            P(DEV),
            P(DEV, None),
            P(DEV),
            P(),
            P(),
            P(DEV, None, None, None, None),
            P(DEV, None, None),
            P(DEV, None, None),
            P(DEV, None, None),
            P(DEV, None),
        ),
        out_specs=(P(DEV, None), P(DEV), P(DEV, None), P(DEV), P(), P()),
        check_vma=False,
    )
```

```python
import functools
import jax
import jax.numpy as jnp
from jax import lax
from jax.experimental import pallas as pl
from jax.experimental.pallas import tpu as pltpu
from jax.sharding import Mesh
from jax.sharding import PartitionSpec as P

D = 256
TILE = 128
TILES = 16
ACTIVE = 16
RELS = 4
LEARN = 0.1
EPS = 1e-6
DEV = ("dev_0", "dev_1", "dev_2", "dev_3")
F32 = jnp.float32
BF16 = jnp.bfloat16


def halves(x):
    hi = x.astype(BF16)
    lo = (x - hi.astype(F32)).astype(BF16)
    return hi, lo


def product(a, b, dims):
    (ah, al), (bh, bl) = a, b
    (ca,), (cb,) = dims
    rows, depth = ah.shape
    if depth == TILE:
        lhs = jnp.concatenate([ah, al, ah], axis=ca)
        rhs = jnp.concatenate([bh, bh, bl], axis=cb)
        return lax.dot_general(lhs, rhs, (dims, ((), ())), preferred_element_type=F32)
    dot = functools.partial(
        lax.dot_general, dimension_numbers=(dims, ((), ())), preferred_element_type=F32
    )
    both = dot(jnp.concatenate([ah, al], axis=0), bh)
    return (both[:rows] + both[rows:]) + dot(ah, bl)


NN = ((1,), (0,))
NT = ((1,), (1,))


def round_kernel(
    turn,
    chained,
    in_place,
    lefts,
    rights,
    kinds,
    counts,
    lstate,
    rstate,
    left_in,
    right_in,
    relations,
    edges,
    *rest,
):
    if chained:
        rel_in, *rest = rest
    (
        left_out,
        lstate_out,
        right_out,
        rstate_out,
        rel_out,
        tl,
        tr,
        gl,
        gr,
        rg,
        mf,
        mh,
        ml,
        ew,
        stl,
        str_,
        hit,
        order,
        num,
        tsem,
        esem,
        msem,
        rsem,
        osem,
        ssem,
    ) = rest
    count = counts[turn]
    pairs = lax.div(count + 1, 2)
    tables = ((tl, left_in, left_out, lefts, gl), (tr, right_in, right_out, rights, gr))

    def tile_load(side, t):
        table, src, *_ = tables[side]
        rows = pl.ds(t * TILE, TILE)
        return pltpu.make_async_copy(src.at[rows, :], table.at[rows, :], tsem.at[side, t])

    def tile_store(side, t):
        table, _, dst, *_ = tables[side]
        rows = pl.ds(t * TILE, TILE)
        return pltpu.make_async_copy(table.at[rows, :], dst.at[rows, :], osem.at[side, t])

    def edge_copy(s):
        return pltpu.make_async_copy(edges.at[turn, s], ew.at[s], esem.at[s])

    rel_load = pltpu.make_async_copy(relations, mf, msem.at[0])
    rel_load.start()
    lines = pl.ds(0, TILES)
    states_in = [
        pltpu.make_async_copy(lstate, stl.at[lines, :], ssem.at[0]),
        pltpu.make_async_copy(rstate, str_.at[lines, :], ssem.at[1]),
    ]
    states_out = [
        pltpu.make_async_copy(stl.at[lines, :], lstate_out, ssem.at[2]),
        pltpu.make_async_copy(str_.at[lines, :], rstate_out, ssem.at[3]),
    ]
    for side in range(2):
        num[side] = 0
        for t in range(TILES):
            hit[side, t] = 0
            order[side, t] = TILES

    def mark(s, _):
        edge_copy(s).start()
        for side in range(2):
            t = tables[side][3][turn, s]

            @pl.when(hit[side, t] == 0)
            def _():
                tile_load(side, t).start()
                hit[side, t] = 1
                order[side, num[side]] = t
                num[side] = num[side] + 1

        return 0

    lax.fori_loop(0, 2 * pairs, mark, 0)
    for copy in states_in:
        copy.start()
    if chained:
        rg_load = pltpu.make_async_copy(rel_in, rg, rsem.at[0])
        rg_load.start()
    else:
        rg[...] = jnp.zeros_like(rg)

    def each_hit(side, act):
        def body(i, _):
            act(order[side, i])
            return 0

        lax.fori_loop(0, num[side], body, 0)

    def each_other(act):
        def body(t, _):
            for side in range(2):

                @pl.when(hit[side, t] == 0)
                def _():
                    act(side, t)

            return 0

        lax.fori_loop(0, TILES, body, 0)

    if not in_place:
        each_other(lambda side, t: tile_load(side, t).start())
    for side, (table, _, _, _, grad) in enumerate(tables):

        def clear(t):
            grad[pl.ds(t * TILE, TILE), :] = jnp.zeros((TILE, D), F32)

        each_hit(side, clear)
        spare = pl.ds(TILES * TILE, TILE)
        grad[spare, :] = jnp.zeros((TILE, D), F32)
        table[spare, :] = jnp.zeros((TILE, D), F32)
    for st in (stl, str_):
        st[pl.ds(TILES, 8), :] = jnp.zeros((8, TILE), F32)
    rel_load.wait()

    def split(r, _):
        hi, lo = halves(mf[r])
        mh[r] = hi
        ml[r] = lo
        return 0

    lax.fori_loop(0, RELS, split, 0)
    for side in range(2):
        each_hit(side, lambda t: tile_load(side, t).wait())
    for copy in states_in:
        copy.wait()
    if chained:
        rg_load.wait()

    def pair(i, _):
        slots = (2 * i, 2 * i + 1)
        for s in slots:
            edge_copy(s).wait()
        at = [lefts[turn, s] * TILE for s in slots]
        bt = [rights[turn, s] * TILE for s in slots]
        kd = [kinds[turn, s] for s in slots]
        live = [jnp.where(s < count, 1.0, 0.0).astype(F32) for s in slots]
        af = [tl[pl.ds(a, TILE), :] for a in at]
        a = [halves(x) for x in af]
        m = [(mh[k], ml[k]) for k in kd]
        p = [halves(product(x, y, NN)) for x, y in zip(a, m)]
        b = [halves(tr[pl.ds(x, TILE), :]) for x in bt]
        s_ = [product(x, y, NT) for x, y in zip(p, b)]
        g = []
        for s, sc, lv in zip(slots, s_, live):
            w = ew[s]
            zero = w == 0
            sc = sc * (D**-0.5)
            sig = jax.nn.sigmoid(jnp.where(zero, sc, -sc))
            coef = jnp.where(zero, 1.0, w.astype(F32) * (-1.0 / 3.0))
            g.append(sig * coef * (lv * D**-0.5))
        gs = [halves(x) for x in g]
        gts = [halves(x.T) for x in g]
        backed = [halves(product(x, y, NN)) for x, y in zip(gs, b)]
        tb = [product(x, y, NN) for x, y in zip(gts, p)]
        ta = [product(x, y, NT) for x, y in zip(backed, m)]
        ats = [halves(x.T) for x in af]
        tm = [product(x, y, NN) for x, y in zip(ats, backed)]
        for j in range(2):
            rows = pl.ds(bt[j], TILE)
            gr[rows, :] += tb[j]
        for j in range(2):
            rows = pl.ds(at[j], TILE)
            gl[rows, :] += ta[j]
        for j in range(2):
            rg[kd[j]] += tm[j]
        return 0

    lax.fori_loop(0, pairs, pair, 0)
    rg_store = pltpu.make_async_copy(rg, rel_out, rsem.at[1])
    rg_store.start()
    if not in_place:

        def pass_on(side, t):
            tile_load(side, t).wait()
            tile_store(side, t).start()

        each_other(pass_on)
    steps = jnp.maximum(num[0], num[1])

    def update(table, grad, st, t):
        rows = pl.ds(t * TILE, TILE)
        g = grad[rows, :]
        mean = jnp.sum(g * g, axis=1, keepdims=True) * (1.0 / D)
        wide = jnp.broadcast_to(st[pl.ds(t, 1), :], (TILE, TILE)).T + mean
        step = LEARN / (jnp.sqrt(wide) + EPS)
        new = table[rows, :] - g * jnp.concatenate([step, step], axis=1)
        return rows, new, wide.T[0:1, :]

    def finish(i, _):
        @pl.when(i < steps)
        def _():
            both = ((tl, gl, stl), (tr, gr, str_))
            at = [order[side, i] for side in range(2)]
            out = [update(*refs, t) for refs, t in zip(both, at)]
            for (table, _, st), t, (rows, new, line) in zip(both, at, out):
                table[rows, :] = new
                st[pl.ds(t, 1), :] = line

        before = jnp.maximum(i - 1, 0)
        for side in range(2):

            @pl.when((i > 0) & (before < num[side]))
            def _():
                tile_store(side, order[side, before]).start()

        return 0

    lax.fori_loop(0, steps + 1, finish, 0)
    for copy in states_out:
        copy.start()
    for side in range(2):
        each_hit(side, lambda t: tile_store(side, t).wait())
    if not in_place:
        each_other(lambda side, t: tile_store(side, t).wait())
    for copy in states_out:
        copy.wait()
    rg_store.wait()


def run_round(turn, ids, left, lstate, right, rstate, relations, edges, rel_grad):
    smem = pl.BlockSpec(memory_space=pltpu.SMEM)
    hbm = pl.BlockSpec(memory_space=pl.ANY)
    rows = TILES * TILE
    args = (*ids, lstate, rstate, left, right, relations, edges)
    specs = [smem] * 4 + [hbm] * 6
    chained = rel_grad is not None
    if chained:
        args += (rel_grad,)
        specs += [hbm]
    return pl.pallas_call(
        functools.partial(round_kernel, turn, chained, chained),
        name="bucket_round",
        out_shape=(
            jax.ShapeDtypeStruct((rows, D), F32),
            jax.ShapeDtypeStruct((TILES, TILE), F32),
            jax.ShapeDtypeStruct((rows, D), F32),
            jax.ShapeDtypeStruct((TILES, TILE), F32),
            jax.ShapeDtypeStruct((RELS, D, D), F32),
        ),
        in_specs=specs,
        out_specs=(hbm,) * 5,
        scratch_shapes=[
            pltpu.VMEM((rows + TILE, D), F32),
            pltpu.VMEM((rows + TILE, D), F32),
            pltpu.VMEM((rows + TILE, D), F32),
            pltpu.VMEM((rows + TILE, D), F32),
            pltpu.VMEM((RELS, D, D), F32),
            pltpu.VMEM((RELS, D, D), F32),
            pltpu.VMEM((RELS, D, D), BF16),
            pltpu.VMEM((RELS, D, D), BF16),
            pltpu.VMEM((ACTIVE, TILE, TILE), jnp.int32),
            pltpu.VMEM((TILES + 8, TILE), F32),
            pltpu.VMEM((TILES + 8, TILE), F32),
            pltpu.SMEM((2, TILES), jnp.int32),
            pltpu.SMEM((2, TILES), jnp.int32),
            pltpu.SMEM((2,), jnp.int32),
            pltpu.SemaphoreType.DMA((2, TILES)),
            pltpu.SemaphoreType.DMA((ACTIVE,)),
            pltpu.SemaphoreType.DMA((1,)),
            pltpu.SemaphoreType.DMA((2,)),
            pltpu.SemaphoreType.DMA((2, TILES)),
            pltpu.SemaphoreType.DMA((4,)),
        ],
        input_output_aliases={6: 0, 7: 2} if chained else {},
        compiler_params=pltpu.CompilerParams(vmem_limit_bytes=62 << 20),
        cost_estimate=pl.CostEstimate(
            flops=2_400_000_000, bytes_accessed=12_000_000, transcendentals=262144
        ),
    )(*args)


AXES = (("dev_0", 8), ("dev_1", 4), ("dev_2", 4), ("dev_3", 2))
PARTS = (6, 3, 2, 3, 2)
MESH = pl.DeviceIdType.MESH


def coordinates(index):
    z = lax.rem(lax.div(index, 32), 8)
    y = lax.rem(lax.div(index, 8), 4)
    x = lax.rem(lax.div(index, 2), 4)
    return (z, y, x, lax.rem(index, 2))


def home_kernel(
    back_left,
    back_right,
    left,
    lstate,
    right,
    rstate,
    grad,
    left_out,
    lstate_out,
    right_out,
    rstate_out,
    total,
    cbuf,
    xacc,
    xbuf,
    zacc,
    zbuf,
    ybuf,
    full,
    home_send,
    home_recv,
    csend,
    crecv,
    ysend,
    yrecv,
    zsend,
    zrecv,
    xsend,
    xrecv,
    tsem,
):
    z, y, x, c = (lax.axis_index(name) for name, _ in AXES)
    me = ((z * 4 + y) * 4 + x) * 2 + c
    count = 256

    def shifted_id(distance):
        return coordinates(lax.rem(me + count + distance, count))

    far = [(lax.rem(z + d, 8), y, x, c) for d in range(1, 8)]
    side = [(z, y, lax.rem(x + d, 4), c) for d in range(1, 4)]
    row = [(z, lax.rem(y + d, 4), x, c) for d in range(1, 4)]
    mate = (z, y, x, 1 - c)
    lines = [shifted_id(d) for d in (back_left, -back_left, back_right, -back_right)]
    peers = lines + [mate] + far + side + row
    barrier = pltpu.get_barrier_semaphore()
    for peer in peers:
        pl.semaphore_signal(barrier, inc=1, device_id=peer, device_id_type=MESH)
    pl.semaphore_wait(barrier, len(peers))

    def send(src, dst, ssem, rsem, peer):
        copy = pltpu.make_async_remote_copy(
            src_ref=src,
            dst_ref=dst,
            send_sem=ssem,
            recv_sem=rsem,
            device_id=peer,
            device_id_type=MESH,
        )
        copy.start()
        return copy

    half = 512
    copies = [
        send(
            grad.at[pl.ds((1 - c) * half, half), :], cbuf, csend.at[0], crecv.at[0], mate
        )
    ]
    homes = [
        send(rstate, rstate_out, home_send.at[0], home_recv.at[0], lines[2]),
        send(lstate, lstate_out, home_send.at[1], home_recv.at[1], lines[0]),
    ]

    def send_home(part):
        rows = pl.ds(sum(PARTS[:part]) * TILE, PARTS[part] * TILE)
        for i, (src, dst, peer) in enumerate(
            ((right, right_out, lines[2]), (left, left_out, lines[0]))
        ):
            at = 2 + 2 * part + i
            homes.append(
                send(src.at[rows, :], dst.at[rows, :], home_send.at[at], home_recv.at[at], peer)
            )

    copies[0].wait()

    def add_core(i, _):
        rows = pl.ds(i * TILE, TILE)
        part = pl.ds(lax.rem(i, 2) * TILE, TILE)
        xacc[lax.div(i, 2), part, :] = grad[pl.ds(c * half + i * TILE, TILE), :] + cbuf[rows, :]
        return 0

    lax.fori_loop(0, 4, add_core, 0)
    inner = (x == 1) | (x == 2)
    mine = lax.rem(x + 3, 4)

    def described(src, dst, ssem, rsem, peer):
        return pltpu.make_async_remote_copy(
            src_ref=src,
            dst_ref=dst,
            send_sem=ssem,
            recv_sem=rsem,
            device_id=peer,
            device_id_type=MESH,
        )

    def to_column(j):
        slot = lax.rem(x - j + 2, 4)
        return described(
            xacc.at[j], xbuf.at[slot], xsend.at[j], xrecv.at[slot], (z, y, 1 + j, c)
        )

    def from_row(slot):
        return described(xbuf.at[slot], xbuf.at[slot], xsend.at[0], xrecv.at[slot], side[0])

    for j in range(2):

        @pl.when(x != 1 + j)
        def _():
            to_column(j).start()

    send_home(0)
    for j in range(2):

        @pl.when(x != 1 + j)
        def _():
            to_column(j).wait_send()

    @pl.when(inner)
    def _():
        for slot in range(3):
            from_row(slot).wait_recv()

        def add_row(i, _):
            rows = pl.ds(i * 32, 32)
            zacc[i] = (xacc[mine, rows, :] + xbuf[0, rows, :]) + (
                xbuf[1, rows, :] + xbuf[2, rows, :]
            )
            return 0

        lax.fori_loop(0, 8, add_row, 0)
        for d, peer in enumerate(far):
            described(zacc.at[peer[0]], zbuf.at[d], zsend.at[d], zrecv.at[d], peer).start()

    send_home(1)

    @pl.when(inner)
    def _():
        for d, peer in enumerate(far):
            described(zacc.at[peer[0]], zbuf.at[d], zsend.at[d], zrecv.at[d], peer).wait()
        own = zacc[z]
        for d in range(7):
            own = own + zbuf[d]
        ybuf[y] = own
        for d, peer in enumerate(row):
            described(ybuf.at[y], ybuf.at[y], ysend.at[d], yrecv.at[d], peer).start()

    send_home(2)

    @pl.when(inner)
    def _():
        for d, peer in enumerate(row):
            described(ybuf.at[y], ybuf.at[y], ysend.at[d], yrecv.at[d], peer).wait()
        full[c, mine, z] = (ybuf[0] + ybuf[1]) + (ybuf[2] + ybuf[3])
        piece = full.at[c, mine, z]
        for d, peer in enumerate(far):
            described(piece, piece, zsend.at[7 + d], zrecv.at[7 + d], peer).start()

    send_home(3)

    def spread(j, d):
        piece = full.at[c, j]
        slot = 3 * j + d
        return described(piece, piece, xsend.at[2 + d], xrecv.at[3 + slot], (z, y, lax.rem(x + 1 + d, 4), c))

    @pl.when(inner)
    def _():
        piece = full.at[c, mine, z]
        for d, peer in enumerate(far):
            described(piece, piece, zsend.at[7 + d], zrecv.at[7 + d], peer).wait()
        for d in range(3):
            spread(mine, d).start()

    send_home(4)

    @pl.when(inner)
    def _():
        for d in range(3):
            spread(mine, d).wait_send()

    for j in range(2):

        @pl.when(x != 1 + j)
        def _():
            spread(j, lax.rem(x - j + 2, 4)).wait_recv()

    piece = full.at[c]
    send(piece, piece, csend.at[1], crecv.at[1], mate).wait()

    out = pltpu.make_async_copy(full, total, tsem.at[0])
    out.start()
    for copy in homes:
        copy.wait()
    out.wait()


def bring_home(back_left, back_right, left, lstate, right, rstate, grad):
    vmem = pl.BlockSpec(memory_space=pltpu.VMEM)
    hbm = pl.BlockSpec(memory_space=pl.ANY)
    like = lambda a: jax.ShapeDtypeStruct(a.shape, a.dtype)
    dma = pltpu.SemaphoreType.DMA
    return pl.pallas_call(
        functools.partial(home_kernel, back_left, back_right),
        name="bring_home",
        out_shape=tuple(like(a) for a in (left, lstate, right, rstate))
        + (jax.ShapeDtypeStruct((2, 2, 8, 32, D), F32),),
        in_specs=[hbm] * 4 + [vmem],
        out_specs=(hbm,) * 5,
        scratch_shapes=[
            pltpu.VMEM((512, D), F32),
            pltpu.VMEM((2, 256, D), F32),
            pltpu.VMEM((3, 256, D), F32),
            pltpu.VMEM((8, 32, D), F32),
            pltpu.VMEM((7, 32, D), F32),
            pltpu.VMEM((4, 32, D), F32),
            pltpu.VMEM((2, 2, 8, 32, D), F32),
            dma((12,)),
            dma((12,)),
            dma((2,)),
            dma((2,)),
            dma((3,)),
            dma((3,)),
            dma((14,)),
            dma((14,)),
            dma((5,)),
            dma((9,)),
            dma((1,)),
        ],
        compiler_params=pltpu.CompilerParams(
            collective_id=0, has_side_effects=True, vmem_limit_bytes=62 << 20
        ),
        cost_estimate=pl.CostEstimate(
            flops=2_000_000, bytes_accessed=12_000_000, transcendentals=1024
        ),
    )(left, lstate, right, rstate, grad)


def settle_kernel(
    left,
    lstate,
    right,
    rstate,
    total,
    rel,
    rel_state,
    left_out,
    lstate_out,
    right_out,
    rstate_out,
    rel_out,
    rel_state_out,
    tl,
    tr,
    sl,
    sr,
    grad,
    old,
    lines,
    isem,
    osem,
    gsem,
    rsem,
    ssem,
):
    parts = 8
    loads = [
        pltpu.make_async_copy(total, grad, gsem.at[0]),
        pltpu.make_async_copy(rel, old, gsem.at[1]),
    ]
    states = [
        pltpu.make_async_copy(lstate, sl, ssem.at[0]),
        pltpu.make_async_copy(rstate, sr, ssem.at[1]),
    ]
    states_back = [
        pltpu.make_async_copy(sl, lstate_out, ssem.at[2]),
        pltpu.make_async_copy(sr, rstate_out, ssem.at[3]),
    ]

    def table_in(side, i):
        rows = pl.ds(i * 256, 256)
        src, dst = ((left, tl), (right, tr))[side]
        return pltpu.make_async_copy(src.at[rows, :], dst.at[rows, :], isem.at[side, i])

    def table_out(side, i):
        rows = pl.ds(i * 256, 256)
        src, dst = ((tl, left_out), (tr, right_out))[side]
        return pltpu.make_async_copy(src.at[rows, :], dst.at[rows, :], osem.at[side, i])

    def rel_store(t):
        rows = pl.ds(t * TILE, TILE)
        return pltpu.make_async_copy(old.at[rows, :], rel_out.at[rows, :], rsem.at[t])

    for copy in loads + states:
        copy.start()

    def begin(i, _):
        table_in(0, i).start()
        table_in(1, i).start()
        return 0

    lax.fori_loop(0, parts, begin, 0)
    for t in range(parts):
        lines[t : t + 1, :] = rel_state[t // 2 : t // 2 + 1, (t % 2) * TILE : (t % 2 + 1) * TILE]
    for copy in loads:
        copy.wait()
    for copy, back in zip(states, states_back):
        copy.wait()
        back.start()

    def update(t, _):
        rows = pl.ds(t * TILE, TILE)
        g = grad[rows, :]
        mean = jnp.sum(g * g, axis=1, keepdims=True) * (1.0 / D)
        wide = jnp.broadcast_to(lines[pl.ds(t, 1), :], (TILE, TILE)).T + mean
        lines[pl.ds(t, 1), :] = wide.T[0:1, :]
        step = LEARN / (jnp.sqrt(wide) + EPS)
        old[rows, :] = old[rows, :] - g * jnp.concatenate([step, step], axis=1)
        for side in range(2):
            table_in(side, t).wait()
            table_out(side, t).start()

        @pl.when(t > 0)
        def _():
            rel_store(t - 1).start()

        return 0

    lax.fori_loop(0, parts, update, 0)
    for t in range(parts):
        rel_state_out[t // 2 : t // 2 + 1, (t % 2) * TILE : (t % 2 + 1) * TILE] = lines[t : t + 1, :]
    rel_store(parts - 1).start()

    def drain(i, _):
        table_out(0, i).wait()
        table_out(1, i).wait()
        rel_store(i).wait()
        return 0

    lax.fori_loop(0, parts, drain, 0)
    for back in states_back:
        back.wait()


def settle(left, lstate, right, rstate, total, rel, rel_state):
    vmem = pl.BlockSpec(memory_space=pltpu.VMEM)
    hbm = pl.BlockSpec(memory_space=pl.ANY)
    like = lambda a: jax.ShapeDtypeStruct(a.shape, a.dtype)
    dma = pltpu.SemaphoreType.DMA
    return pl.pallas_call(
        settle_kernel,
        name="settle",
        out_shape=tuple(like(a) for a in (left, lstate, right, rstate, rel, rel_state)),
        in_specs=[hbm] * 6 + [vmem],
        out_specs=(hbm,) * 5 + (vmem,),
        scratch_shapes=[
            pltpu.VMEM(left.shape, F32),
            pltpu.VMEM(right.shape, F32),
            pltpu.VMEM(lstate.shape, F32),
            pltpu.VMEM(rstate.shape, F32),
            pltpu.VMEM(rel.shape, F32),
            pltpu.VMEM(rel.shape, F32),
            pltpu.VMEM((8, TILE), F32),
            dma((2, 8)),
            dma((2, 8)),
            dma((2,)),
            dma((8,)),
            dma((4,)),
        ],
        compiler_params=pltpu.CompilerParams(vmem_limit_bytes=62 << 20),
        cost_estimate=pl.CostEstimate(
            flops=2_000_000, bytes_accessed=12_000_000, transcendentals=1024
        ),
    )(left, lstate, right, rstate, total, rel, rel_state)


def shifted(block, axis, distance):
    devices = range(lax.axis_size(axis))
    route = [((i - distance) % len(devices), i) for i in devices]
    return lax.ppermute(block, axis, route)


def per_device(
    left_table,
    left_state,
    right_table,
    right_state,
    relations,
    relation_state,
    edge_weights,
    tile_left,
    tile_right,
    tile_relation,
    live_count,
):
    edges = edge_weights[0]
    ids = (tile_left[0], tile_right[0], tile_relation[0], live_count[0])
    rounds = edges.shape[0]
    last = rounds - 1
    packed = jnp.concatenate([x[last].reshape(-1) for x in ids])
    last_edges, packed = shifted((edges[last:], packed), DEV, -1)
    rel_grad = None
    table_left, state_left = left_table, left_state.reshape(TILES, TILE)
    table_right, state_right = right_table, right_state.reshape(TILES, TILE)
    for turn in range(last):
        table_left, state_left, table_right, state_right, rel_grad = run_round(
            turn, ids, table_left, state_left, table_right, state_right, relations, edges, rel_grad
        )
        if turn + 1 < last:
            table_right, state_right = shifted((table_right, state_right), DEV, 1)
        if turn == 0:
            table_right, last_edges, packed = lax.optimization_barrier(
                (table_right, last_edges, packed)
            )
    last_ids = [packed[i * ACTIVE : (i + 1) * ACTIVE].reshape(1, ACTIVE) for i in range(3)]
    last_ids.append(packed[3 * ACTIVE :])
    table_left, state_left = shifted((table_left, state_left), DEV, -1)
    table_left, state_left, table_right, state_right, rel_grad = run_round(
        0, last_ids, table_left, state_left, table_right, state_right, relations, last_edges, rel_grad
    )
    kinds_count, width = (relations.shape[0], relations.shape[1])
    *home, total = bring_home(
        1,
        1 - last,
        table_left,
        state_left,
        table_right,
        state_right,
        rel_grad.reshape(kinds_count * width, width),
    )
    table_left, state_left, table_right, state_right, new_rel, new_state = settle(
        *home,
        total.reshape(kinds_count * width, width),
        relations.reshape(kinds_count * width, width),
        relation_state,
    )
    return (
        table_left,
        state_left.reshape(-1),
        table_right,
        state_right.reshape(-1),
        new_rel.reshape(kinds_count, width, width),
        new_state,
    )


def solution(mesh):
    torus = Mesh(mesh.devices.reshape(8, 4, 4, 2), ("dev_0", "dev_1", "dev_2", "dev_3"))
    return jax.shard_map(
        per_device,
        mesh=torus,
        in_specs=(
            P(DEV, None),
            P(DEV),
            P(DEV, None),
            P(DEV),
            P(),
            P(),
            P(DEV, None, None, None, None),
            P(DEV, None, None),
            P(DEV, None, None),
            P(DEV, None, None),
            P(DEV, None),
        ),
        out_specs=(P(DEV, None), P(DEV), P(DEV, None), P(DEV), P(), P()),
        check_vma=False,
    )
```

```python
import functools
import jax
import jax.numpy as jnp
from jax import lax
from jax.experimental import pallas as pl
from jax.experimental.pallas import tpu as pltpu
from jax.sharding import Mesh
from jax.sharding import PartitionSpec as P

D = 256
TILE = 128
TILES = 16
ACTIVE = 16
RELS = 4
LEARN = 0.1
EPS = 1e-6
DEV = ("dev_0", "dev_1", "dev_2", "dev_3")
F32 = jnp.float32
BF16 = jnp.bfloat16


def halves(x):
    hi = x.astype(BF16)
    lo = (x - hi.astype(F32)).astype(BF16)
    return hi, lo


def product(a, b, dims):
    (ah, al), (bh, bl) = a, b
    (ca,), (cb,) = dims
    rows, depth = ah.shape
    if depth == TILE:
        lhs = jnp.concatenate([ah, al, ah], axis=ca)
        rhs = jnp.concatenate([bh, bh, bl], axis=cb)
        return lax.dot_general(lhs, rhs, (dims, ((), ())), preferred_element_type=F32)
    dot = functools.partial(
        lax.dot_general, dimension_numbers=(dims, ((), ())), preferred_element_type=F32
    )
    both = dot(jnp.concatenate([ah, al], axis=0), bh)
    return (both[:rows] + both[rows:]) + dot(ah, bl)


NN = ((1,), (0,))
NT = ((1,), (1,))


def round_kernel(
    turn,
    chained,
    in_place,
    lefts,
    rights,
    kinds,
    counts,
    lstate,
    rstate,
    left_in,
    right_in,
    relations,
    edges,
    *rest,
):
    if chained:
        rel_in, *rest = rest
    (
        left_out,
        lstate_out,
        right_out,
        rstate_out,
        rel_out,
        tl,
        tr,
        gl,
        gr,
        rg,
        mf,
        mh,
        ml,
        ew,
        stl,
        str_,
        hit,
        order,
        num,
        tsem,
        esem,
        msem,
        rsem,
        osem,
        ssem,
    ) = rest
    count = counts[turn]
    pairs = lax.div(count + 1, 2)
    tables = ((tl, left_in, left_out, lefts, gl), (tr, right_in, right_out, rights, gr))

    def tile_load(side, t):
        table, src, *_ = tables[side]
        rows = pl.ds(t * TILE, TILE)
        return pltpu.make_async_copy(src.at[rows, :], table.at[rows, :], tsem.at[side, t])

    def tile_store(side, t):
        table, _, dst, *_ = tables[side]
        rows = pl.ds(t * TILE, TILE)
        return pltpu.make_async_copy(table.at[rows, :], dst.at[rows, :], osem.at[side, t])

    def edge_copy(s):
        return pltpu.make_async_copy(edges.at[turn, s], ew.at[s], esem.at[s])

    rel_load = pltpu.make_async_copy(relations, mf, msem.at[0])
    rel_load.start()
    lines = pl.ds(0, TILES)
    states_in = [
        pltpu.make_async_copy(lstate, stl.at[lines, :], ssem.at[0]),
        pltpu.make_async_copy(rstate, str_.at[lines, :], ssem.at[1]),
    ]
    states_out = [
        pltpu.make_async_copy(stl.at[lines, :], lstate_out, ssem.at[2]),
        pltpu.make_async_copy(str_.at[lines, :], rstate_out, ssem.at[3]),
    ]
    for side in range(2):
        num[side] = 0
        for t in range(TILES):
            hit[side, t] = 0
            order[side, t] = TILES

    def mark(s, _):
        edge_copy(s).start()
        for side in range(2):
            t = tables[side][3][turn, s]

            @pl.when(hit[side, t] == 0)
            def _():
                tile_load(side, t).start()
                hit[side, t] = 1
                order[side, num[side]] = t
                num[side] = num[side] + 1

        return 0

    lax.fori_loop(0, 2 * pairs, mark, 0)
    for copy in states_in:
        copy.start()
    if chained:
        rg_load = pltpu.make_async_copy(rel_in, rg, rsem.at[0])
        rg_load.start()
    else:
        rg[...] = jnp.zeros_like(rg)

    def each_hit(side, act):
        def body(i, _):
            act(order[side, i])
            return 0

        lax.fori_loop(0, num[side], body, 0)

    def each_other(act):
        def body(t, _):
            for side in range(2):

                @pl.when(hit[side, t] == 0)
                def _():
                    act(side, t)

            return 0

        lax.fori_loop(0, TILES, body, 0)

    if not in_place:
        each_other(lambda side, t: tile_load(side, t).start())
    for side, (table, _, _, _, grad) in enumerate(tables):

        def clear(t):
            grad[pl.ds(t * TILE, TILE), :] = jnp.zeros((TILE, D), F32)

        each_hit(side, clear)
        spare = pl.ds(TILES * TILE, TILE)
        grad[spare, :] = jnp.zeros((TILE, D), F32)
        table[spare, :] = jnp.zeros((TILE, D), F32)
    for st in (stl, str_):
        st[pl.ds(TILES, 8), :] = jnp.zeros((8, TILE), F32)
    rel_load.wait()

    def split(r, _):
        hi, lo = halves(mf[r])
        mh[r] = hi
        ml[r] = lo
        return 0

    lax.fori_loop(0, RELS, split, 0)
    for side in range(2):
        each_hit(side, lambda t: tile_load(side, t).wait())
    for copy in states_in:
        copy.wait()
    if chained:
        rg_load.wait()

    def pair(i, _):
        slots = (2 * i, 2 * i + 1)
        for s in slots:
            edge_copy(s).wait()
        at = [lefts[turn, s] * TILE for s in slots]
        bt = [rights[turn, s] * TILE for s in slots]
        kd = [kinds[turn, s] for s in slots]
        live = [jnp.where(s < count, 1.0, 0.0).astype(F32) for s in slots]
        af = [tl[pl.ds(a, TILE), :] for a in at]
        a = [halves(x) for x in af]
        m = [(mh[k], ml[k]) for k in kd]
        p = [halves(product(x, y, NN)) for x, y in zip(a, m)]
        b = [halves(tr[pl.ds(x, TILE), :]) for x in bt]
        s_ = [product(x, y, NT) for x, y in zip(p, b)]
        g = []
        for s, sc, lv in zip(slots, s_, live):
            w = ew[s]
            zero = w == 0
            sc = sc * (D**-0.5)
            sig = jax.nn.sigmoid(jnp.where(zero, sc, -sc))
            coef = jnp.where(zero, 1.0, w.astype(F32) * (-1.0 / 3.0))
            g.append(sig * coef * (lv * D**-0.5))
        gs = [halves(x) for x in g]
        gts = [halves(x.T) for x in g]
        backed = [halves(product(x, y, NN)) for x, y in zip(gs, b)]
        tb = [product(x, y, NN) for x, y in zip(gts, p)]
        ta = [product(x, y, NT) for x, y in zip(backed, m)]
        ats = [halves(x.T) for x in af]
        tm = [product(x, y, NN) for x, y in zip(ats, backed)]
        for j in range(2):
            rows = pl.ds(bt[j], TILE)
            gr[rows, :] += tb[j]
        for j in range(2):
            rows = pl.ds(at[j], TILE)
            gl[rows, :] += ta[j]
        for j in range(2):
            rg[kd[j]] += tm[j]
        return 0

    lax.fori_loop(0, pairs, pair, 0)
    rg_store = pltpu.make_async_copy(rg, rel_out, rsem.at[1])
    rg_store.start()
    if not in_place:

        def pass_on(side, t):
            tile_load(side, t).wait()
            tile_store(side, t).start()

        each_other(pass_on)
    steps = jnp.maximum(num[0], num[1])

    def update(table, grad, st, t):
        rows = pl.ds(t * TILE, TILE)
        g = grad[rows, :]
        mean = jnp.sum(g * g, axis=1, keepdims=True) * (1.0 / D)
        wide = jnp.broadcast_to(st[pl.ds(t, 1), :], (TILE, TILE)).T + mean
        step = LEARN / (jnp.sqrt(wide) + EPS)
        new = table[rows, :] - g * jnp.concatenate([step, step], axis=1)
        return rows, new, wide.T[0:1, :]

    def finish(i, _):
        @pl.when(i < steps)
        def _():
            both = ((tl, gl, stl), (tr, gr, str_))
            at = [order[side, i] for side in range(2)]
            out = [update(*refs, t) for refs, t in zip(both, at)]
            for (table, _, st), t, (rows, new, line) in zip(both, at, out):
                table[rows, :] = new
                st[pl.ds(t, 1), :] = line

        before = jnp.maximum(i - 1, 0)
        for side in range(2):

            @pl.when((i > 0) & (before < num[side]))
            def _():
                tile_store(side, order[side, before]).start()

        return 0

    lax.fori_loop(0, steps + 1, finish, 0)
    for copy in states_out:
        copy.start()
    for side in range(2):
        each_hit(side, lambda t: tile_store(side, t).wait())
    if not in_place:
        each_other(lambda side, t: tile_store(side, t).wait())
    for copy in states_out:
        copy.wait()
    rg_store.wait()


def run_round(turn, ids, left, lstate, right, rstate, relations, edges, rel_grad):
    smem = pl.BlockSpec(memory_space=pltpu.SMEM)
    hbm = pl.BlockSpec(memory_space=pl.ANY)
    rows = TILES * TILE
    args = (*ids, lstate, rstate, left, right, relations, edges)
    specs = [smem] * 4 + [hbm] * 6
    chained = rel_grad is not None
    if chained:
        args += (rel_grad,)
        specs += [hbm]
    return pl.pallas_call(
        functools.partial(round_kernel, turn, chained, chained),
        name="bucket_round",
        out_shape=(
            jax.ShapeDtypeStruct((rows, D), F32),
            jax.ShapeDtypeStruct((TILES, TILE), F32),
            jax.ShapeDtypeStruct((rows, D), F32),
            jax.ShapeDtypeStruct((TILES, TILE), F32),
            jax.ShapeDtypeStruct((RELS, D, D), F32),
        ),
        in_specs=specs,
        out_specs=(hbm,) * 5,
        scratch_shapes=[
            pltpu.VMEM((rows + TILE, D), F32),
            pltpu.VMEM((rows + TILE, D), F32),
            pltpu.VMEM((rows + TILE, D), F32),
            pltpu.VMEM((rows + TILE, D), F32),
            pltpu.VMEM((RELS, D, D), F32),
            pltpu.VMEM((RELS, D, D), F32),
            pltpu.VMEM((RELS, D, D), BF16),
            pltpu.VMEM((RELS, D, D), BF16),
            pltpu.VMEM((ACTIVE, TILE, TILE), jnp.int32),
            pltpu.VMEM((TILES + 8, TILE), F32),
            pltpu.VMEM((TILES + 8, TILE), F32),
            pltpu.SMEM((2, TILES), jnp.int32),
            pltpu.SMEM((2, TILES), jnp.int32),
            pltpu.SMEM((2,), jnp.int32),
            pltpu.SemaphoreType.DMA((2, TILES)),
            pltpu.SemaphoreType.DMA((ACTIVE,)),
            pltpu.SemaphoreType.DMA((1,)),
            pltpu.SemaphoreType.DMA((2,)),
            pltpu.SemaphoreType.DMA((2, TILES)),
            pltpu.SemaphoreType.DMA((4,)),
        ],
        input_output_aliases={6: 0, 7: 2} if chained else {},
        compiler_params=pltpu.CompilerParams(vmem_limit_bytes=62 << 20),
        cost_estimate=pl.CostEstimate(
            flops=2_400_000_000, bytes_accessed=12_000_000, transcendentals=262144
        ),
    )(*args)


AXES = (("dev_0", 8), ("dev_1", 4), ("dev_2", 4), ("dev_3", 2))
PARTS = (2, 3, 3, 2, 3, 3)
MESH = pl.DeviceIdType.MESH


def coordinates(index):
    z = lax.rem(lax.div(index, 32), 8)
    y = lax.rem(lax.div(index, 8), 4)
    x = lax.rem(lax.div(index, 2), 4)
    return (z, y, x, lax.rem(index, 2))


def home_kernel(
    back_left,
    back_right,
    left,
    lstate,
    right,
    rstate,
    grad,
    left_out,
    lstate_out,
    right_out,
    rstate_out,
    total,
    cbuf,
    xacc,
    xbuf,
    zacc,
    zbuf,
    ybuf,
    full,
    home_send,
    home_recv,
    csend,
    crecv,
    ysend,
    yrecv,
    zsend,
    zrecv,
    xsend,
    xrecv,
    tsem,
):
    z, y, x, c = (lax.axis_index(name) for name, _ in AXES)
    me = ((z * 4 + y) * 4 + x) * 2 + c
    count = 256

    def shifted_id(distance):
        return coordinates(lax.rem(me + count + distance, count))

    far = [(lax.rem(z + d, 8), y, x, c) for d in range(1, 8)]
    side = [(z, y, lax.rem(x + d, 4), c) for d in range(1, 4)]
    row = [(z, lax.rem(y + d, 4), x, c) for d in range(1, 4)]
    mate = (z, y, x, 1 - c)
    lines = [shifted_id(d) for d in (back_left, -back_left, back_right, -back_right)]
    peers = lines + [mate] + far + side + row
    barrier = pltpu.get_barrier_semaphore()
    for peer in peers:
        pl.semaphore_signal(barrier, inc=1, device_id=peer, device_id_type=MESH)
    pl.semaphore_wait(barrier, len(peers))

    def send(src, dst, ssem, rsem, peer):
        copy = pltpu.make_async_remote_copy(
            src_ref=src,
            dst_ref=dst,
            send_sem=ssem,
            recv_sem=rsem,
            device_id=peer,
            device_id_type=MESH,
        )
        copy.start()
        return copy

    half = 512
    copies = [
        send(
            grad.at[pl.ds((1 - c) * half, half), :], cbuf, csend.at[0], crecv.at[0], mate
        )
    ]
    homes = [
        send(rstate, rstate_out, home_send.at[0], home_recv.at[0], lines[2]),
        send(lstate, lstate_out, home_send.at[1], home_recv.at[1], lines[0]),
    ]

    def send_home(part):
        rows = pl.ds(sum(PARTS[:part]) * TILE, PARTS[part] * TILE)
        for i, (src, dst, peer) in enumerate(
            ((right, right_out, lines[2]), (left, left_out, lines[0]))
        ):
            at = 2 + 2 * part + i
            homes.append(
                send(src.at[rows, :], dst.at[rows, :], home_send.at[at], home_recv.at[at], peer)
            )

    send_home(0)
    copies[0].wait()

    def add_core(i, _):
        rows = pl.ds(i * TILE, TILE)
        part = pl.ds(lax.rem(i, 2) * TILE, TILE)
        xacc[lax.div(i, 2), part, :] = grad[pl.ds(c * half + i * TILE, TILE), :] + cbuf[rows, :]
        return 0

    lax.fori_loop(0, 4, add_core, 0)
    inner = (x == 1) | (x == 2)
    mine = lax.rem(x + 3, 4)

    def described(src, dst, ssem, rsem, peer):
        return pltpu.make_async_remote_copy(
            src_ref=src,
            dst_ref=dst,
            send_sem=ssem,
            recv_sem=rsem,
            device_id=peer,
            device_id_type=MESH,
        )

    def to_column(j):
        slot = lax.rem(x - j + 2, 4)
        return described(
            xacc.at[j], xbuf.at[slot], xsend.at[j], xrecv.at[slot], (z, y, 1 + j, c)
        )

    def from_row(slot):
        return described(xbuf.at[slot], xbuf.at[slot], xsend.at[0], xrecv.at[slot], side[0])

    for j in range(2):

        @pl.when(x != 1 + j)
        def _():
            to_column(j).start()

    send_home(1)
    @pl.when(inner)
    def _():
        for slot in range(3):
            from_row(slot).wait_recv()

        def add_row(i, _):
            rows = pl.ds(i * 32, 32)
            zacc[i] = (xacc[mine, rows, :] + xbuf[0, rows, :]) + (
                xbuf[1, rows, :] + xbuf[2, rows, :]
            )
            return 0

        lax.fori_loop(0, 8, add_row, 0)
        for d, peer in enumerate(far):
            described(zacc.at[peer[0]], zbuf.at[d], zsend.at[d], zrecv.at[d], peer).start()

    send_home(2)

    @pl.when(inner)
    def _():
        for d, peer in enumerate(far):
            described(zacc.at[peer[0]], zbuf.at[d], zsend.at[d], zrecv.at[d], peer).wait()
        own = zacc[z]
        for d in range(7):
            own = own + zbuf[d]
        ybuf[y] = own
        for d, peer in enumerate(row):
            described(ybuf.at[y], ybuf.at[y], ysend.at[d], yrecv.at[d], peer).start()

    send_home(3)

    @pl.when(inner)
    def _():
        for d, peer in enumerate(row):
            described(ybuf.at[y], ybuf.at[y], ysend.at[d], yrecv.at[d], peer).wait()
        full[c, mine, z] = (ybuf[0] + ybuf[1]) + (ybuf[2] + ybuf[3])
        piece = full.at[c, mine, z]
        for d, peer in enumerate(far):
            described(piece, piece, zsend.at[7 + d], zrecv.at[7 + d], peer).start()

    send_home(4)

    def spread(j, d):
        piece = full.at[c, j]
        slot = 3 * j + d
        return described(piece, piece, xsend.at[2 + d], xrecv.at[3 + slot], (z, y, lax.rem(x + 1 + d, 4), c))

    @pl.when(inner)
    def _():
        piece = full.at[c, mine, z]
        for d, peer in enumerate(far):
            described(piece, piece, zsend.at[7 + d], zrecv.at[7 + d], peer).wait()
        for d in range(3):
            spread(mine, d).start()

    send_home(5)

    for j in range(2):

        @pl.when(x != 1 + j)
        def _():
            spread(j, lax.rem(x - j + 2, 4)).wait_recv()

    piece = full.at[c]
    send(piece, piece, csend.at[1], crecv.at[1], mate).wait()
    for j in range(2):

        @pl.when(x != 1 + j)
        def _():
            to_column(j).wait_send()

    @pl.when(inner)
    def _():
        for d in range(3):
            spread(mine, d).wait_send()


    out = pltpu.make_async_copy(full, total, tsem.at[0])
    out.start()
    for copy in homes:
        copy.wait()
    out.wait()


def bring_home(back_left, back_right, left, lstate, right, rstate, grad):
    vmem = pl.BlockSpec(memory_space=pltpu.VMEM)
    hbm = pl.BlockSpec(memory_space=pl.ANY)
    like = lambda a: jax.ShapeDtypeStruct(a.shape, a.dtype)
    dma = pltpu.SemaphoreType.DMA
    return pl.pallas_call(
        functools.partial(home_kernel, back_left, back_right),
        name="bring_home",
        out_shape=tuple(like(a) for a in (left, lstate, right, rstate))
        + (jax.ShapeDtypeStruct((2, 2, 8, 32, D), F32),),
        in_specs=[hbm] * 4 + [vmem],
        out_specs=(hbm,) * 5,
        scratch_shapes=[
            pltpu.VMEM((512, D), F32),
            pltpu.VMEM((2, 256, D), F32),
            pltpu.VMEM((3, 256, D), F32),
            pltpu.VMEM((8, 32, D), F32),
            pltpu.VMEM((7, 32, D), F32),
            pltpu.VMEM((4, 32, D), F32),
            pltpu.VMEM((2, 2, 8, 32, D), F32),
            dma((14,)),
            dma((14,)),
            dma((2,)),
            dma((2,)),
            dma((3,)),
            dma((3,)),
            dma((14,)),
            dma((14,)),
            dma((5,)),
            dma((9,)),
            dma((1,)),
        ],
        compiler_params=pltpu.CompilerParams(
            collective_id=0, has_side_effects=True, vmem_limit_bytes=62 << 20
        ),
        cost_estimate=pl.CostEstimate(
            flops=2_000_000, bytes_accessed=12_000_000, transcendentals=1024
        ),
    )(left, lstate, right, rstate, grad)


def settle_kernel(
    left,
    lstate,
    right,
    rstate,
    total,
    rel,
    rel_state,
    left_out,
    lstate_out,
    right_out,
    rstate_out,
    rel_out,
    rel_state_out,
    tl,
    tr,
    sl,
    sr,
    grad,
    old,
    lines,
    isem,
    osem,
    gsem,
    rsem,
    ssem,
):
    parts = 8
    loads = [
        pltpu.make_async_copy(total, grad, gsem.at[0]),
        pltpu.make_async_copy(rel, old, gsem.at[1]),
    ]
    states = [
        pltpu.make_async_copy(lstate, sl, ssem.at[0]),
        pltpu.make_async_copy(rstate, sr, ssem.at[1]),
    ]
    states_back = [
        pltpu.make_async_copy(sl, lstate_out, ssem.at[2]),
        pltpu.make_async_copy(sr, rstate_out, ssem.at[3]),
    ]

    def table_in(side, i):
        rows = pl.ds(i * 256, 256)
        src, dst = ((left, tl), (right, tr))[side]
        return pltpu.make_async_copy(src.at[rows, :], dst.at[rows, :], isem.at[side, i])

    def table_out(side, i):
        rows = pl.ds(i * 256, 256)
        src, dst = ((tl, left_out), (tr, right_out))[side]
        return pltpu.make_async_copy(src.at[rows, :], dst.at[rows, :], osem.at[side, i])

    def rel_store(t):
        rows = pl.ds(t * TILE, TILE)
        return pltpu.make_async_copy(old.at[rows, :], rel_out.at[rows, :], rsem.at[t])

    for copy in loads + states:
        copy.start()

    def begin(i, _):
        table_in(0, i).start()
        table_in(1, i).start()
        return 0

    lax.fori_loop(0, parts, begin, 0)
    for t in range(parts):
        lines[t : t + 1, :] = rel_state[t // 2 : t // 2 + 1, (t % 2) * TILE : (t % 2 + 1) * TILE]
    for copy in loads:
        copy.wait()
    for copy, back in zip(states, states_back):
        copy.wait()
        back.start()

    def update(t, _):
        rows = pl.ds(t * TILE, TILE)
        g = grad[rows, :]
        mean = jnp.sum(g * g, axis=1, keepdims=True) * (1.0 / D)
        wide = jnp.broadcast_to(lines[pl.ds(t, 1), :], (TILE, TILE)).T + mean
        lines[pl.ds(t, 1), :] = wide.T[0:1, :]
        step = LEARN / (jnp.sqrt(wide) + EPS)
        old[rows, :] = old[rows, :] - g * jnp.concatenate([step, step], axis=1)
        for side in range(2):
            table_in(side, t).wait()
            table_out(side, t).start()

        @pl.when(t > 0)
        def _():
            rel_store(t - 1).start()

        return 0

    lax.fori_loop(0, parts, update, 0)
    for t in range(parts):
        rel_state_out[t // 2 : t // 2 + 1, (t % 2) * TILE : (t % 2 + 1) * TILE] = lines[t : t + 1, :]
    rel_store(parts - 1).start()

    def drain(i, _):
        table_out(0, i).wait()
        table_out(1, i).wait()
        rel_store(i).wait()
        return 0

    lax.fori_loop(0, parts, drain, 0)
    for back in states_back:
        back.wait()


def settle(left, lstate, right, rstate, total, rel, rel_state):
    vmem = pl.BlockSpec(memory_space=pltpu.VMEM)
    hbm = pl.BlockSpec(memory_space=pl.ANY)
    like = lambda a: jax.ShapeDtypeStruct(a.shape, a.dtype)
    dma = pltpu.SemaphoreType.DMA
    return pl.pallas_call(
        settle_kernel,
        name="settle",
        out_shape=tuple(like(a) for a in (left, lstate, right, rstate, rel, rel_state)),
        in_specs=[hbm] * 6 + [vmem],
        out_specs=(hbm,) * 5 + (vmem,),
        scratch_shapes=[
            pltpu.VMEM(left.shape, F32),
            pltpu.VMEM(right.shape, F32),
            pltpu.VMEM(lstate.shape, F32),
            pltpu.VMEM(rstate.shape, F32),
            pltpu.VMEM(rel.shape, F32),
            pltpu.VMEM(rel.shape, F32),
            pltpu.VMEM((8, TILE), F32),
            dma((2, 8)),
            dma((2, 8)),
            dma((2,)),
            dma((8,)),
            dma((4,)),
        ],
        compiler_params=pltpu.CompilerParams(vmem_limit_bytes=62 << 20),
        cost_estimate=pl.CostEstimate(
            flops=2_000_000, bytes_accessed=12_000_000, transcendentals=1024
        ),
    )(left, lstate, right, rstate, total, rel, rel_state)


def shifted(block, axis, distance):
    devices = range(lax.axis_size(axis))
    route = [((i - distance) % len(devices), i) for i in devices]
    return lax.ppermute(block, axis, route)


def per_device(
    left_table,
    left_state,
    right_table,
    right_state,
    relations,
    relation_state,
    edge_weights,
    tile_left,
    tile_right,
    tile_relation,
    live_count,
):
    edges = edge_weights[0]
    ids = (tile_left[0], tile_right[0], tile_relation[0], live_count[0])
    rounds = edges.shape[0]
    last = rounds - 1
    packed = jnp.concatenate([x[last].reshape(-1) for x in ids])
    last_edges, packed = shifted((edges[last:], packed), DEV, -1)
    rel_grad = None
    table_left, state_left = left_table, left_state.reshape(TILES, TILE)
    table_right, state_right = right_table, right_state.reshape(TILES, TILE)
    for turn in range(last):
        table_left, state_left, table_right, state_right, rel_grad = run_round(
            turn, ids, table_left, state_left, table_right, state_right, relations, edges, rel_grad
        )
        if turn + 1 < last:
            table_right, state_right = shifted((table_right, state_right), DEV, 1)
        if turn == 0:
            table_right, last_edges, packed = lax.optimization_barrier(
                (table_right, last_edges, packed)
            )
    last_ids = [packed[i * ACTIVE : (i + 1) * ACTIVE].reshape(1, ACTIVE) for i in range(3)]
    last_ids.append(packed[3 * ACTIVE :])
    table_left, state_left = shifted((table_left, state_left), DEV, -1)
    table_left, state_left, table_right, state_right, rel_grad = run_round(
        0, last_ids, table_left, state_left, table_right, state_right, relations, last_edges, rel_grad
    )
    kinds_count, width = (relations.shape[0], relations.shape[1])
    *home, total = bring_home(
        1,
        1 - last,
        table_left,
        state_left,
        table_right,
        state_right,
        rel_grad.reshape(kinds_count * width, width),
    )
    table_left, state_left, table_right, state_right, new_rel, new_state = settle(
        *home,
        total.reshape(kinds_count * width, width),
        relations.reshape(kinds_count * width, width),
        relation_state,
    )
    return (
        table_left,
        state_left.reshape(-1),
        table_right,
        state_right.reshape(-1),
        new_rel.reshape(kinds_count, width, width),
        new_state,
    )


def solution(mesh):
    torus = Mesh(mesh.devices.reshape(8, 4, 4, 2), ("dev_0", "dev_1", "dev_2", "dev_3"))
    return jax.shard_map(
        per_device,
        mesh=torus,
        in_specs=(
            P(DEV, None),
            P(DEV),
            P(DEV, None),
            P(DEV),
            P(),
            P(),
            P(DEV, None, None, None, None),
            P(DEV, None, None),
            P(DEV, None, None),
            P(DEV, None, None),
            P(DEV, None),
        ),
        out_specs=(P(DEV, None), P(DEV), P(DEV, None), P(DEV), P(), P()),
        check_vma=False,
    )
```
